32 devices in a mesh: tm: 8 (over z, x), region: 4 (over y, core).
Axes of the slice: x: 2, y: 2, z: 4, core: 2. Of those that a mesh axis runs over, the one named last changes fastest.
Arguments:
- solution: float32 [1024, 4096], P('tm', 'region'), may hold values from -6 to 6
- residual: float32 [1024, 4096], P('tm', 'region'), may hold values from -50 to 50
- direction: float32 [1024, 4096], P('tm', 'region'), may hold values from -50 to 50
- decay: float32 [1024, 4096], P('tm', 'region'), may hold values from 0 to 1, as said below
- spatial: bfloat16 [4096, 4096], P('region'), may hold values from -1 to 2, as said below
- tiles: bfloat16 [8, 4, 8, 128, 512], P('tm', 'region'), may hold values from -0.1875 to 0.1875
- tile_block: int32 [8, 4, 8], P('tm', 'region'), may hold values from 0 to 7
- tile_time: int32 [8, 4, 8], P('tm', 'region'), may hold values from 0 to 383
- tile_cell: int32 [8, 4, 8], P('tm', 'region'), may hold values from 0 to 1
- tile_count: int32 [8, 4], P('tm', 'region'), may hold values from 1 to 8, as said below
- noise_inv: float32 [64, 128], P('tm'), may hold values from 0.25 to 2
Outputs:
- solution_new: float32 [1024, 4096], P('tm', 'region')
- residual_new: float32 [1024, 4096], P('tm', 'region')
- direction_new: float32 [1024, 4096], P('tm', 'region')
The draws below stay inside these ranges and needn't reach their ends.
Inputs may be any that keep to these rules, and one draw needn't show every extreme that they name: Slots 0 to tile_count - 1 of a window and region hold tiles, the rest are padding; some window and region has 8. `decay`: strictly between 0 and 1. `spatial`: symmetric.
All inputs are finite; a program needn't handle non-finite values.
Results may differ from the reference program's by a relative error of at most 0.0028.
Values may be sent and summed in bfloat16 or wider, within the bound.
No kernel may reach another device: no remote copies, remote signals or barrier semaphores. Data moves between devices by JAX's collectives and lax.ppermute only.
A program may use at most 64 MiB of HBM per device.

```python
import math
import jax
import jax.numpy as jnp
from jax import lax

FB = 512
SB = 128
RC = 1024
TW = 128
NSB = 8
TCAP = 8
BACK = 2
WINDOWS = 8
REGIONS = 4
EMISSION_EPOCHS = 1024
CELLS = 4096
SPAN = 384
CBLK = 2


def scaled_field(key):
    key_a, key_b = jax.random.split(key)
    ramp_up = jnp.arange(EMISSION_EPOCHS, dtype=jnp.float32) / max(EMISSION_EPOCHS - 1, 1)
    row_scale = 10.0 ** ramp_up
    entries = jnp.clip(jax.random.normal(key_a, (EMISSION_EPOCHS, CELLS), jnp.float32), -5.0, 5.0)
    col_scale = 10.0 ** jax.random.uniform(key_b, (CELLS,), jnp.float32)
    return entries * row_scale[:, None] * col_scale[None, :] / 10.0


def draw_residual(key, part):
    return scaled_field(jax.random.fold_in(key, 11))


def draw_direction(key, part):
    return scaled_field(jax.random.fold_in(key, 23))


def draw_decay(key, part):
    key_a, key_b, key_c, key_d, sampler_seed_number5, key_f = jax.random.split(key, 6)
    slow_share = 0.5
    is_slow = jax.random.uniform(key_a, (CELLS,), jnp.float32) < slow_share
    slow_rate = jnp.exp(jax.random.uniform(key_b, (CELLS,), jnp.float32, math.log(0.1), math.log(0.8))) / EMISSION_EPOCHS
    fast_rate = jnp.exp(jax.random.uniform(key_c, (CELLS,), jnp.float32, math.log(1.0 / 40.0), math.log(0.2)))
    base_rate = jnp.where(is_slow, slow_rate, fast_rate)
    jitter = jax.random.uniform(key_d, (EMISSION_EPOCHS, CELLS), jnp.float32, 0.5, 1.5)
    decay_val = jnp.exp(-base_rate[None, :] * jitter)
    pulse_onset_index = jax.random.randint(sampler_seed_number5, (2,), 0, EMISSION_EPOCHS)
    cut_indices = jax.random.uniform(key_f, (2, CELLS), jnp.float32, 0.6, 0.8)
    epoch_index = jnp.arange(EMISSION_EPOCHS)[:, None]
    front_cut_index = jnp.where(epoch_index == pulse_onset_index[0], cut_indices[0][None, :], 1.0)
    rear_cut_index = jnp.where(epoch_index == pulse_onset_index[1], cut_indices[1][None, :], 1.0)
    return decay_val * front_cut_index * rear_cut_index


def draw_spatial(key, part):
    key_a, key_b = jax.random.split(key)
    entries = jnp.clip(jax.random.normal(key_a, (CELLS, CELLS), jnp.float32), -5.0, 5.0)
    symmetric = (entries + entries.T) / math.sqrt(2.0)
    diag_gain = jax.random.uniform(key_b, (CELLS,), jnp.float32, 1.0, 1.5)
    return (jnp.eye(CELLS, dtype=jnp.float32) * diag_gain[None, :] + 0.5 * symmetric / math.sqrt(CELLS)).astype(jnp.bfloat16)


def draw_tile_count(key, part):
    key_a, key_b = jax.random.split(key)
    counts = jax.random.randint(key_a, (WINDOWS, REGIONS), TCAP // 8, TCAP * 5 // 8 + 1)
    chosen_dev = jax.random.randint(key_b, (), 0, WINDOWS * REGIONS)
    flat_ids = jnp.arange(WINDOWS * REGIONS).reshape(WINDOWS, REGIONS)
    return jnp.where(flat_ids == chosen_dev, TCAP, counts).astype(jnp.int32)


def place_ends(values, rng, smallest, largest):
    longest = values.shape.index(max(values.shape))
    spots = []
    for shift in (0, 1):
        where = [jax.random.randint(jax.random.fold_in(rng, axis), (), 0, length) for axis, length in enumerate(values.shape)]
        where[longest] = (where[longest] + shift) % values.shape[longest]
        spots.append(tuple(where))
    return values.at[spots[0]].set(smallest).at[spots[1]].set(largest)


def steps_of(own_key, extent, cuts, smallest, high):
    loudness = 1.0
    for position, parts in cuts:
        draws = jax.random.uniform(jax.random.fold_in(jax.random.fold_in(own_key, 6), position), (parts,), jnp.float32, smallest / len(cuts), high / len(cuts))
        loudness = loudness * jnp.repeat(jnp.exp(draws), extent[position] // parts).reshape((-1,) + (1,) * (len(extent) - 1 - position))
    return loudness


def bell_draw(stream_key, extent, scale, limit, shards=(), held_as=jnp.bfloat16):
    gain = steps_of(stream_key, extent, shards, -0.22, 0.18) if shards else 1.0
    result = jax.random.normal(stream_key, extent, jnp.float32) * scale * gain
    return jnp.minimum(jnp.maximum(result, -limit), limit).astype(held_as)


def setup_inputs(seed: int = 0) -> dict:
    arg_keys = jax.random.split(jax.random.key(seed), 12)
    solution = bell_draw(arg_keys[0], (EMISSION_EPOCHS, CELLS), 1.0, 6.0, ((0, 8), (1, 4)), jnp.float32)
    residual = draw_residual(jax.random.fold_in(arg_keys[11], 71), 0)
    direction = draw_direction(jax.random.fold_in(arg_keys[11], 71), 0)
    decay = draw_decay(jax.random.fold_in(arg_keys[11], 71), 0)
    spatial = draw_spatial(jax.random.fold_in(arg_keys[11], 71), 0)
    tiles = bell_draw(arg_keys[5], (WINDOWS, REGIONS, TCAP, SB, FB), (2 * FB) ** -0.5, 0.1875, ((0, 8), (1, 4)))
    tile_block = place_ends(jax.random.randint(arg_keys[6], (WINDOWS, REGIONS, TCAP), 0, NSB), jax.random.fold_in(arg_keys[6], 1), 0, NSB - 1).astype(jnp.int32)
    tile_time = place_ends(jax.random.randint(arg_keys[7], (WINDOWS, REGIONS, TCAP), 0, SPAN), jax.random.fold_in(arg_keys[7], 1), 0, SPAN - 1).astype(jnp.int32)
    tile_cell = place_ends(jax.random.randint(arg_keys[8], (WINDOWS, REGIONS, TCAP), 0, CBLK), jax.random.fold_in(arg_keys[8], 1), 0, CBLK - 1).astype(jnp.int32)
    tile_count = draw_tile_count(jax.random.fold_in(arg_keys[11], 71), 0)
    noise_inv = jnp.clip(jnp.exp(math.log(2.0) - 2.0794415 * jax.random.uniform(arg_keys[10], (WINDOWS * NSB, SB), jnp.float32) ** steps_of(arg_keys[10], (WINDOWS * NSB, SB), ((0, 8),), -0.2, 0.2)), 0.25, 2.0)
    return dict(solution=solution, residual=residual, direction=direction, decay=decay, spatial=spatial, tiles=tiles, tile_block=tile_block, tile_time=tile_time, tile_cell=tile_cell, tile_count=tile_count, noise_inv=noise_inv)


def reference(solution, residual, direction, decay, spatial, tiles, tile_block, tile_time, tile_cell, tile_count, noise_inv):
    precise = lax.Precision.HIGHEST
    gain_in = jnp.sqrt(1.0 - decay * decay)
    spatial_wide = spatial.astype(jnp.float32)
    dir_half = direction.astype(jnp.bfloat16)
    mixed_cells = jnp.dot(dir_half.astype(jnp.float32), spatial_wide.T, precision=precise, preferred_element_type=jnp.float32)

    def forward_step(state, inputs):
        state = inputs[0] * state + inputs[1]
        return (state, state)
    zero_row = jnp.zeros((CELLS,), jnp.float32)
    _, filtered = lax.scan(forward_step, zero_row, (decay, gain_in * mixed_cells))
    coarse = filtered.astype(jnp.bfloat16)
    padded = jnp.concatenate([jnp.zeros((BACK * TW, CELLS), jnp.bfloat16), coarse], axis=0)
    span_len = (BACK + 1) * TW
    cell_blocks = RC // FB
    slot_ids = jnp.arange(TCAP, dtype=jnp.int32)
    block_ids = jnp.arange(NSB, dtype=jnp.int32)
    place_ids = jnp.arange(span_len * cell_blocks, dtype=jnp.int32)

    def window_obs(window_idx):
        window = lax.dynamic_slice_in_dim(padded, (window_idx * TW).astype(jnp.int32), span_len, 0)
        running = jnp.zeros((NSB, SB), jnp.float32)
        for region in range(REGIONS):
            cells_of = window[:, region * RC:(region + 1) * RC].reshape(span_len, cell_blocks, FB)
            is_live = slot_ids < tile_count[window_idx, region]
            chosen = cells_of[tile_time[window_idx, region], tile_cell[window_idx, region]].astype(jnp.float32)
            partial_value = jnp.einsum('jkc,jc->jk', tiles[window_idx, region].astype(jnp.float32), chosen, precision=precise)
            onehot = ((tile_block[window_idx, region][None, :] == block_ids[:, None]) & is_live[None, :]).astype(jnp.float32)
            running = running + jnp.dot(onehot, partial_value, precision=precise)
        return running
    observed = lax.map(window_obs, jnp.arange(WINDOWS, dtype=jnp.int32))
    weighted = (observed.reshape(WINDOWS * NSB, SB) * noise_inv).astype(jnp.bfloat16).reshape(WINDOWS, NSB, SB)

    def window_back(accum, window_idx):
        columns = []
        for region in range(REGIONS):
            is_live = slot_ids < tile_count[window_idx, region]
            picked = weighted[window_idx][tile_block[window_idx, region]].astype(jnp.float32)
            partial_value = jnp.einsum('jkc,jk->jc', tiles[window_idx, region].astype(jnp.float32), picked, precision=precise)
            epoch_index = tile_time[window_idx, region] * cell_blocks + tile_cell[window_idx, region]
            onehot = ((epoch_index[None, :] == place_ids[:, None]) & is_live[None, :]).astype(jnp.float32)
            columns.append(jnp.dot(onehot, partial_value, precision=precise).reshape(span_len, RC))
        block_sum = jnp.concatenate(columns, axis=1)
        first_row = (window_idx * TW).astype(jnp.int32)
        current = lax.dynamic_slice_in_dim(accum, first_row, span_len, 0)
        accum = lax.dynamic_update_slice_in_dim(accum, current + block_sum, first_row, 0)
        return (accum, None)
    accum, _ = lax.scan(window_back, jnp.zeros((EMISSION_EPOCHS + BACK * TW, CELLS), jnp.float32), jnp.arange(WINDOWS, dtype=jnp.int32))
    adjoint = accum[BACK * TW:]

    def backward_step(carry, inputs):
        held_sum = inputs[1] + carry
        return (inputs[0] * held_sum, held_sum)
    _, held_sum = lax.scan(backward_step, zero_row, (decay, adjoint), reverse=True)
    pulled = (gain_in * held_sum).astype(jnp.bfloat16)
    spread = jnp.dot(pulled.astype(jnp.float32), spatial_wide, precision=precise, preferred_element_type=jnp.float32)
    op_image = direction + spread
    norm_old = jnp.sum(residual * residual)
    curvature = jnp.sum(direction * op_image)
    step_len = norm_old / curvature
    solution_new = solution + step_len * direction
    residual_new = residual - step_len * op_image
    norm_new = jnp.sum(residual_new * residual_new)
    direction_new = residual_new + norm_new / norm_old * direction
    return (solution_new, residual_new, direction_new)
```

```python
import jax
import jax.numpy as jnp
from jax import lax
from jax.experimental import pallas as pl
from jax.experimental.pallas import tpu as pltpu
from jax.sharding import PartitionSpec as P

FB = 512
BACK = 2
STRIP = 256
SUB = 8
LANES = 128


VMEM = pl.BlockSpec(memory_space=pltpu.VMEM)
SMEM = pl.BlockSpec(memory_space=pltpu.SMEM)


def swapped(block, axis, bit):
    return lax.ppermute(block, axis, [(i, i ^ bit) for i in range(lax.axis_size(axis))])


def shifted(block, axis, distance):
    devices = range(lax.axis_size(axis))
    route = [(i - distance, i) for i in devices if i - distance in devices]
    return lax.ppermute(block, axis, route)


def region_blocks(block):
    blocks, bit = {0: block}, lax.axis_size("region") // 2
    while bit:
        blocks.update({k ^ bit: swapped(b, "region", bit) for k, b in list(blocks.items())})
        bit //= 2
    return blocks


def window_rows(rows):
    bit = 1
    while bit < lax.axis_size("tm"):
        rows = jnp.concatenate([rows, swapped(rows, "tm", bit)], axis=0)
        bit *= 2
    return rows


def nt_dot(a, b):
    return lax.dot_general(a, b, (((1,), (1,)), ((), ())), preferred_element_type=jnp.float32)


def strided(start, steps):
    return pl.ds(start, steps // SUB, stride=SUB)


def lanes(k):
    return slice(k * LANES, (k + 1) * LANES)


def to_columns(columns, value):
    for k in range(value.shape[1] // LANES):
        columns[k] = value[:, lanes(k)]


def decay_kernel(places, decay_ref, rows_ref, end_ref, local, carried):
    steps, width = decay_ref.shape
    tiles = steps // SUB
    to_columns(local, decay_ref[...])
    for k in range(width // LANES):
        running = local[k, strided(0, steps), :]
        for s in range(1, SUB):
            running = running * local[k, strided(s, steps), :]
            local[k, strided(s, steps), :] = running
        state = jnp.ones((1, LANES), jnp.float32)
        for b in range(tiles):
            carried[k, b : b + 1, :] = state
            state = state * running[b : b + 1, :]
        end_ref[:, lanes(k)] = state
    capacity = rows_ref.shape[0] // (BACK + 1)
    for reader in range(BACK + 1):
        for slot in range(capacity):
            step = places[reader, 1, slot]
            first = places[reader, 2, slot] * (FB // LANES)
            row = reader * capacity + slot
            for k in range(FB // LANES):
                rows_ref[row : row + 1, lanes(k)] = (
                    local[first + k, pl.ds(step, 1), :]
                    * carried[first + k, pl.ds(step // SUB, 1), :]
                )


def decay_rows(places, decay):
    steps, width = decay.shape
    rows = places.shape[0] * places.shape[2]
    return pl.pallas_call(
        decay_kernel,
        out_shape=(
            jax.ShapeDtypeStruct((rows, FB), jnp.float32),
            jax.ShapeDtypeStruct((1, width), jnp.float32),
        ),
        in_specs=[SMEM, VMEM],
        out_specs=(VMEM, VMEM),
        scratch_shapes=[
            pltpu.VMEM((width // LANES, steps, LANES), jnp.float32),
            pltpu.VMEM((width // LANES, steps // SUB, LANES), jnp.float32),
        ],
        name="decay_rows",
    )(places, decay)


def first_kernel(regions, a_ref, b_ref, s_a, s_b, out_ref):
    out_ref[...] = nt_dot(a_ref[...], s_a[...]) + nt_dot(b_ref[...], s_b[...])


def spatial_specs(width, count):
    return [
        pl.BlockSpec((STRIP, width), lambda i, regions, k=k: (i, regions[k])) for k in range(count)
    ]


def whole(shape):
    return pl.BlockSpec(shape, lambda i, regions: (0,) * len(shape))


def first_products(regions, a, b, spatial):
    steps, width = a.shape
    return pl.pallas_call(
        first_kernel,
        out_shape=jax.ShapeDtypeStruct((steps, spatial.shape[0]), jnp.float32),
        grid_spec=pltpu.PrefetchScalarGridSpec(
            num_scalar_prefetch=1,
            grid=(spatial.shape[0] // STRIP,),
            in_specs=[whole(a.shape), whole(b.shape)] + spatial_specs(width, 2),
            out_specs=pl.BlockSpec((steps, STRIP), lambda i, regions: (0, i)),
        ),
        name="first_products",
    )(regions, a, b, spatial, spatial)


def filter_kernel(
    regions, places, a_ref, b_ref, s_a, s_b, part_ref, decay_ref, rows_ref, end_ref, decays, local
):
    steps = a_ref.shape[0]
    tiles = steps // SUB
    strip = pl.program_id(0)
    mixed = part_ref[...] + nt_dot(a_ref[...], s_a[...]) + nt_dot(b_ref[...], s_b[...])
    decay = decay_ref[...]
    driven = jnp.sqrt(1.0 - decay * decay) * mixed
    to_columns(decays, decay)
    for k in range(STRIP // LANES):
        column = strip * (STRIP // LANES) + k
        local[column] = driven[:, lanes(k)]
        state = local[column, strided(0, steps), :]
        factor = decays[k, strided(0, steps), :]
        states, factors = [state], [factor]
        for s in range(1, SUB):
            step_decay = decays[k, strided(s, steps), :]
            state = step_decay * state + local[column, strided(s, steps), :]
            factor = step_decay * factor
            states.append(state)
            factors.append(factor)
        carry = jnp.zeros((1, LANES), jnp.float32)
        entering = []
        for b in range(tiles):
            entering.append(carry)
            carry = factor[b : b + 1, :] * carry + state[b : b + 1, :]
        end_ref[:, lanes(k)] = carry
        entering = jnp.concatenate(entering, axis=0)
        for s in range(SUB):
            local[column, strided(s, steps), :] = states[s] + factors[s] * entering

    @pl.when(strip == pl.num_programs(0) - 1)
    def _():
        capacity = rows_ref.shape[0] // (BACK + 1)
        for reader in range(BACK + 1):
            for slot in range(capacity):
                step = places[reader, 1, slot]
                first = places[reader, 2, slot] * (FB // LANES)
                row = reader * capacity + slot
                for k in range(FB // LANES):
                    rows_ref[row : row + 1, lanes(k)] = local[first + k, pl.ds(step, 1), :]


def filter_rows(regions, places, a, b, spatial, part, decay):
    steps, width = a.shape
    rows = places.shape[0] * places.shape[2]
    strips = width // STRIP

    def strip_spec(height):
        return pl.BlockSpec((height, STRIP), lambda i, *_: (0, i))

    def all_of(shape):
        return pl.BlockSpec(shape, lambda i, *_: (0,) * len(shape))

    return pl.pallas_call(
        filter_kernel,
        out_shape=(
            jax.ShapeDtypeStruct((rows, FB), jnp.float32),
            jax.ShapeDtypeStruct((1, width), jnp.float32),
        ),
        grid_spec=pltpu.PrefetchScalarGridSpec(
            num_scalar_prefetch=2,
            grid=(strips,),
            in_specs=[
                all_of(a.shape),
                all_of(b.shape),
                pl.BlockSpec((STRIP, width), lambda i, regions, places: (i, regions[0])),
                pl.BlockSpec((STRIP, width), lambda i, regions, places: (i, regions[1])),
                strip_spec(steps),
                strip_spec(steps),
            ],
            out_specs=(all_of((rows, FB)), strip_spec(1)),
            scratch_shapes=[
                pltpu.VMEM((STRIP // LANES, steps, LANES), jnp.float32),
                pltpu.VMEM((width // LANES, steps, LANES), jnp.float32),
            ],
        ),
        name="filter_rows",
    )(regions, places, a, b, spatial, spatial, part, decay)


def observe_kernel(
    here, places, ends_ref, own_ref, near_ref, far_ref, tiles_ref, seen_ref, factor_ref, entered, picked
):
    capacity, soundings, cells = tiles_ref.shape
    windows = ends_ref.shape[0] // 2
    width = ends_ref.shape[1]
    own = here[0]
    entered[...] = jnp.zeros_like(entered)

    def one(window, state):
        for back in range(BACK + 1):

            @pl.when(window == own - back)
            def _():
                entered[BACK - back : BACK - back + 1, :] = state

        row = 2 * (window ^ own)
        return ends_ref[pl.ds(row, 1), :] * state + ends_ref[pl.ds(row + 1, 1), :]

    lax.fori_loop(0, windows, one, jnp.zeros((1, width), jnp.float32), unroll=windows <= 8)
    for slot in range(capacity):
        which = places[0, 0, slot]
        columns = pl.ds(pl.multiple_of(places[0, 2, slot] * FB, FB), FB)
        row = pl.ds(slot, 1)
        later = pl.ds(capacity + slot, 1)
        offset = jnp.where(
            which == 2, own_ref[row, :], jnp.where(which == 1, near_ref[row, :], far_ref[row, :])
        )
        factor = jnp.where(
            which == 2, own_ref[later, :], jnp.where(which == 1, near_ref[later, :], far_ref[later, :])
        )
        factor_ref[row, :] = factor
        value = offset + factor * entered[pl.ds(which, 1), columns]
        picked[row, :] = jnp.where(places[0, 3, slot] == 1, value, 0.0)
    rows = picked[...].astype(jnp.bfloat16)
    products = nt_dot(rows, tiles_ref[...].reshape(capacity * soundings, cells))
    blocks = lax.broadcasted_iota(jnp.int32, seen_ref.shape, 0)
    seen = jnp.zeros(seen_ref.shape, jnp.float32)
    for slot in range(capacity):
        part = products[slot : slot + 1, slot * soundings : (slot + 1) * soundings]
        seen = seen + jnp.where(blocks == places[0, 4, slot], part, 0.0)
    seen_ref[...] = seen


def observe(here, places, ends, own, near, far, tiles, block_count):
    capacity, soundings, cells = tiles.shape
    return pl.pallas_call(
        observe_kernel,
        out_shape=(
            jax.ShapeDtypeStruct((block_count, soundings), jnp.float32),
            jax.ShapeDtypeStruct((capacity, cells), jnp.float32),
        ),
        in_specs=[SMEM, SMEM] + [VMEM] * 5,
        out_specs=(VMEM, VMEM),
        scratch_shapes=[
            pltpu.VMEM((SUB, ends.shape[1]), jnp.float32),
            pltpu.VMEM((capacity, cells), jnp.float32),
        ],
        name="observe",
    )(here, places, ends, own, near, far, tiles)


def adjoint_kernel(places, seen_ref, other_ref, noise_ref, tiles_ref, factor_ref, rows_ref, sums_ref, weights):
    capacity, soundings, cells = tiles_ref.shape
    observed = seen_ref[...] + other_ref[...]
    weights[...] = (observed * noise_ref[...]).astype(jnp.bfloat16).astype(jnp.float32)
    slots = lax.broadcasted_iota(jnp.int32, (capacity, soundings), 0)
    pieces = []
    for slot in range(capacity):
        picked = weights[pl.ds(places[0, 4, slot], 1), :]
        pieces.append(jnp.where((slots == slot) & (places[0, 3, slot] == 1), picked, 0.0))
    spread = jnp.concatenate(pieces, axis=1).astype(jnp.bfloat16)
    rows = jnp.dot(
        spread,
        tiles_ref[...].reshape(capacity * soundings, cells),
        preferred_element_type=jnp.float32,
    )
    rows_ref[...] = rows
    handed = rows * factor_ref[...]
    sums_ref[...] = jnp.zeros_like(sums_ref)
    for slot in range(capacity):
        columns = pl.ds(pl.multiple_of(places[0, 2, slot] * FB, FB), FB)
        which = pl.ds(places[0, 0, slot], 1)
        sums_ref[which, columns] = sums_ref[which, columns] + handed[slot : slot + 1, :]


def adjoint_rows(places, seen, other, noise, tiles, factors, width):
    capacity, soundings, cells = tiles.shape
    return pl.pallas_call(
        adjoint_kernel,
        out_shape=(
            jax.ShapeDtypeStruct((capacity, cells), jnp.float32),
            jax.ShapeDtypeStruct((SUB, width), jnp.float32),
        ),
        in_specs=[SMEM] + [VMEM] * 5,
        out_specs=(VMEM, VMEM),
        scratch_shapes=[pltpu.VMEM(noise.shape, jnp.float32)],
        name="adjoint_rows",
    )(places, seen, other, noise, tiles, factors)


def hold_kernel(
    here, places, ends_ref, sums_ref, own_ref, near_ref, far_ref, decay_ref, pulled_ref, decays, terms
):
    steps, width = decay_ref.shape
    tiles = steps // SUB
    capacity = own_ref.shape[0]
    windows = ends_ref.shape[0] // 2
    own = here[0]

    def one(hop, state):
        window = windows - 1 - hop
        arriving = jnp.zeros((1, width), jnp.float32)
        for ahead in range(BACK + 1):
            reader = jnp.minimum(window + ahead, windows - 1)
            row = (reader ^ own) * SUB + BACK - ahead
            arriving = arriving + jnp.where(
                window + ahead < windows, sums_ref[pl.ds(row, 1), :], 0.0
            )
        passed = ends_ref[pl.ds(2 * (window ^ own), 1), :] * state + arriving
        return jnp.where(window > own, passed, state)

    incoming = lax.fori_loop(
        0, windows - 1, one, jnp.zeros((1, width), jnp.float32), unroll=windows <= 8
    )
    terms[...] = jnp.zeros_like(terms)
    to_columns(decays, decay_ref[...])
    for reader, rows in enumerate((own_ref, near_ref, far_ref)):
        for slot in range(capacity):
            mine = (places[reader, 0, slot] == BACK - reader) & (places[reader, 3, slot] == 1)
            first = places[reader, 2, slot] * (FB // LANES)
            step = pl.ds(places[reader, 1, slot], 1)
            for k in range(FB // LANES):
                terms[first + k, step, :] = terms[first + k, step, :] + jnp.where(
                    mine, rows[slot : slot + 1, lanes(k)], 0.0
                )
    for k in range(width // LANES):
        state = terms[k, strided(SUB - 1, steps), :]
        factor = jnp.ones_like(state)
        states, factors = [state], [factor]
        for s in range(SUB - 2, -1, -1):
            step_decay = decays[k, strided(s + 1, steps), :]
            state = terms[k, strided(s, steps), :] + step_decay * state
            factor = step_decay * factor
            states.append(state)
            factors.append(factor)
        first = decays[k, strided(0, steps), :]
        state, factor = first * state, first * factor
        carry = incoming[:, lanes(k)]
        entering = []
        for b in range(tiles - 1, -1, -1):
            entering.insert(0, carry)
            carry = state[b : b + 1, :] + factor[b : b + 1, :] * carry
        entering = jnp.concatenate(entering, axis=0)
        for s in range(SUB):
            terms[k, strided(SUB - 1 - s, steps), :] = states[s] + factors[s] * entering
        decay = decays[k]
        pulled_ref[:, lanes(k)] = (jnp.sqrt(1.0 - decay * decay) * terms[k]).astype(jnp.bfloat16)


def hold(here, places, ends, sums, own, near, far, decay):
    steps, width = decay.shape
    return pl.pallas_call(
        hold_kernel,
        out_shape=jax.ShapeDtypeStruct((steps, width), jnp.bfloat16),
        in_specs=[SMEM, SMEM] + [VMEM] * 6,
        out_specs=VMEM,
        scratch_shapes=[
            pltpu.VMEM((width // LANES, steps, LANES), jnp.float32),
            pltpu.VMEM((width // LANES, steps, LANES), jnp.float32),
        ],
        name="hold",
    )(here, places, ends, sums, own, near, far, decay)


def image_kernel(
    regions, a_ref, b_ref, s_a, s_b, part_ref, direction_ref, residual_ref, image_ref, sums_ref
):
    strip = pl.program_id(0)
    direction = direction_ref[...]
    residual = residual_ref[...]
    image = direction + (
        part_ref[...] + nt_dot(a_ref[...], s_a[...]) + nt_dot(b_ref[...], s_b[...])
    )
    image_ref[...] = image
    shares = [
        jnp.sum(term, axis=0, keepdims=True)
        for term in (residual * residual, direction * image, residual * image, image * image)
    ]

    @pl.when(strip == 0)
    def _():
        sums_ref[...] = jnp.zeros_like(sums_ref)

    sums_ref[0:4, :] = sums_ref[0:4, :] + jnp.concatenate(shares, axis=0)


def make_image(regions, a, b, spatial, part, direction, residual):
    steps, width = a.shape
    strip_spec = pl.BlockSpec((steps, STRIP), lambda i, regions: (0, i))
    return pl.pallas_call(
        image_kernel,
        out_shape=(
            jax.ShapeDtypeStruct((steps, width), jnp.float32),
            jax.ShapeDtypeStruct((SUB, STRIP), jnp.float32),
        ),
        grid_spec=pltpu.PrefetchScalarGridSpec(
            num_scalar_prefetch=1,
            grid=(width // STRIP,),
            in_specs=[whole(a.shape), whole(b.shape)]
            + spatial_specs(width, 2)
            + [strip_spec, strip_spec, strip_spec],
            out_specs=(strip_spec, whole((SUB, STRIP))),
        ),
        name="make_image",
    )(regions, a, b, spatial, spatial, part, direction, residual)


def body(
    solution,
    residual,
    direction,
    decay,
    spatial,
    tiles,
    tile_block,
    tile_time,
    tile_cell,
    tile_count,
    noise_inv,
):
    window_len, row_width = direction.shape
    footprint = tiles[0, 0]
    capacity = footprint.shape[0]
    block_count = noise_inv.shape[0]
    here = lax.axis_index("tm").astype(jnp.int32).reshape(1)
    region = lax.axis_index("region").astype(jnp.int32)
    live = (jnp.arange(capacity, dtype=jnp.int32) < tile_count[0, 0]).astype(jnp.int32)
    place = jnp.stack(
        [
            tile_time[0, 0] // window_len,
            tile_time[0, 0] % window_len,
            tile_cell[0, 0],
            live,
            tile_block[0, 0],
        ]
    )
    dir_half = direction.astype(jnp.bfloat16)
    blocks = region_blocks(dir_half)
    order = sorted(blocks)
    near_regions = jnp.stack([region ^ k for k in order[:2]])
    far_regions = jnp.stack([region ^ k for k in order[2:]])
    places = jnp.stack([place] + [shifted(place, "tm", -hop) for hop in range(1, BACK + 1)])
    factor_rows, factor_end = decay_rows(places, decay)
    part = first_products(near_regions, blocks[order[0]], blocks[order[1]], spatial)
    offset_rows, offset_end = filter_rows(
        far_regions, places, blocks[order[2]], blocks[order[3]], spatial, part, decay
    )

    def for_reader(k):
        at = slice(k * capacity, (k + 1) * capacity)
        return jnp.concatenate([offset_rows[at], factor_rows[at]], axis=0)

    arrived = [shifted(for_reader(hop), "tm", hop) for hop in range(1, BACK + 1)]
    ends = window_rows(jnp.concatenate([factor_end, offset_end], axis=0))
    seen, factors = observe(
        here, places, ends, for_reader(0), arrived[0], arrived[1], footprint, block_count
    )
    bit = 1
    while bit < lax.axis_size("region") // 2:
        seen = seen + swapped(seen, "region", bit)
        bit *= 2
    other = swapped(seen, "region", bit)
    rows, sums = adjoint_rows(places, seen, other, noise_inv, footprint, factors, row_width)
    returned = [shifted(rows, "tm", -hop) for hop in range(1, BACK + 1)]
    pulled = hold(
        here, places, ends, window_rows(sums), rows, returned[0], returned[1], decay
    )
    blocks = region_blocks(pulled)
    part = first_products(near_regions, blocks[order[0]], blocks[order[1]], spatial)
    op_image, shares = make_image(
        far_regions, blocks[order[2]], blocks[order[3]], spatial, part, direction, residual
    )
    totals = jnp.sum(shares, axis=1, keepdims=True) + jnp.zeros((1, 128), jnp.float32)
    for axis in ("region", "tm"):
        bit = 1
        while bit < lax.axis_size(axis):
            totals = totals + swapped(totals, axis, bit)
            bit *= 2
    norm_old, curvature, cross_sum, image_sq = (totals[k, 0] for k in range(4))
    step_len = norm_old / curvature
    residual_new = residual - step_len * op_image
    norm_new = norm_old - 2.0 * step_len * cross_sum + step_len * step_len * image_sq
    solution_new = solution + step_len * direction
    direction_new = residual_new + norm_new / norm_old * direction
    return (solution_new, residual_new, direction_new)


def solution(mesh):
    return jax.shard_map(
        body,
        mesh=mesh,
        in_specs=(
            P("tm", "region"),
            P("tm", "region"),
            P("tm", "region"),
            P("tm", "region"),
            P("region", None),
            P("tm", "region", None, None, None),
            P("tm", "region", None),
            P("tm", "region", None),
            P("tm", "region", None),
            P("tm", "region"),
            P("tm", None),
        ),
        out_specs=(P("tm", "region"), P("tm", "region"), P("tm", "region")),
        check_vma=False,
    )
```

```python
import jax
import jax.numpy as jnp
from jax import lax
from jax.experimental import pallas as pl
from jax.experimental.pallas import tpu as pltpu
from jax.sharding import PartitionSpec as P

FB = 512
BACK = 2
STRIP = 256
SUB = 8
LANES = 128
KERNEL_VMEM = 12 * 2**20


def swapped(block, axis, bit):
    return lax.ppermute(block, axis, [(i, i ^ bit) for i in range(lax.axis_size(axis))])


def shifted(block, axis, distance):
    devices = range(lax.axis_size(axis))
    route = [(i - distance, i) for i in devices if i - distance in devices]
    return lax.ppermute(block, axis, route)


def region_blocks(block):
    blocks, bit = {0: block}, lax.axis_size("region") // 2
    while bit:
        blocks.update({k ^ bit: swapped(b, "region", bit) for k, b in list(blocks.items())})
        bit //= 2
    return blocks


def window_rows(rows):
    bit, pieces = 1, [rows]
    while bit < lax.axis_size("tm"):
        joined = jnp.concatenate(pieces, axis=0) if len(pieces) > 1 else rows
        pieces.append(swapped(joined, "tm", bit))
        bit *= 2
    return pieces


def nt_dot(a, b):
    return lax.dot_general(a, b, (((1,), (1,)), ((), ())), preferred_element_type=jnp.float32)


def strided(start, steps):
    return pl.ds(start, steps // SUB, stride=SUB)


def lanes(k):
    return slice(k * LANES, (k + 1) * LANES)


def to_columns(columns, value):
    for k in range(value.shape[1] // LANES):
        columns[k] = value[:, lanes(k)]


def on_chip(kernel, scalars, arrays, outs, scratch=(), name=None, out_spaces=None):
    spaces = out_spaces or [pltpu.VMEM] * len(outs)
    results = pl.pallas_call(
        kernel,
        out_shape=tuple(space(shape, dtype) for space, (shape, dtype) in zip(spaces, outs)),
        in_specs=[pl.BlockSpec(memory_space=pltpu.SMEM)] * len(scalars)
        + [pl.BlockSpec(memory_space=pltpu.VMEM)] * len(arrays),
        out_specs=tuple(pl.BlockSpec(memory_space=pltpu.VMEM) for _ in outs),
        scratch_shapes=list(scratch),
        compiler_params=pltpu.CompilerParams(vmem_limit_bytes=KERNEL_VMEM),
        name=name,
    )(*scalars, *(pltpu.with_memory_space_constraint(a, pltpu.VMEM) for a in arrays))
    return results


def tile_at(place, slot, steps, capacity):
    time = place[slot]
    return time // steps, time % steps, place[capacity + slot] * (FB // LANES)


def decay_kernel(own, near, far, decay_ref, rows_ref, end_ref, local, carried):
    steps, width = decay_ref.shape
    tiles = steps // SUB
    to_columns(local, decay_ref[...])
    for k in range(width // LANES):
        running = local[k, strided(0, steps), :]
        for s in range(1, SUB):
            running = running * local[k, strided(s, steps), :]
            local[k, strided(s, steps), :] = running
        state = jnp.ones((1, LANES), jnp.float32)
        for b in range(tiles):
            carried[k, b : b + 1, :] = state
            state = state * running[b : b + 1, :]
        end_ref[:, lanes(k)] = state
    capacity = rows_ref.shape[0] // (BACK + 1)
    for reader, place in enumerate((own, near, far)):
        for slot in range(capacity):
            _, step, first = tile_at(place, slot, steps, capacity)
            row = reader * capacity + slot
            for k in range(FB // LANES):
                rows_ref[row : row + 1, lanes(k)] = (
                    local[first + k, pl.ds(step, 1), :]
                    * carried[first + k, pl.ds(step // SUB, 1), :]
                )


def product(block, place, region, spatial, strip):
    width = block.shape[1]
    columns = pl.ds(pl.multiple_of((region[0] ^ place) * width, width), width)
    return nt_dot(block[...], spatial[strip * STRIP : (strip + 1) * STRIP, columns])


def first_kernel(region, a_ref, b_ref, spatial, out_ref):
    for strip in range(out_ref.shape[1] // STRIP):
        out_ref[:, strip * STRIP : (strip + 1) * STRIP] = product(
            a_ref, 0, region, spatial, strip
        ) + product(b_ref, 1, region, spatial, strip)


def filter_kernel(
    region,
    own,
    near,
    far,
    a_ref,
    b_ref,
    spatial,
    part_ref,
    decay_ref,
    factors_ref,
    last_ref,
    own_ref,
    near_ref,
    far_ref,
    end_ref,
    decays,
    local,
):
    steps, width = a_ref.shape
    tiles = steps // SUB
    capacity = own_ref.shape[0] // 2
    to_columns(decays, decay_ref[...])
    end_ref[0:1, :] = last_ref[...]
    for strip in range(width // STRIP):
        mixed = (
            part_ref[:, strip * STRIP : (strip + 1) * STRIP]
            + product(a_ref, 2, region, spatial, strip)
            + product(b_ref, 3, region, spatial, strip)
        )
        for k in range(strip * STRIP // LANES, (strip + 1) * STRIP // LANES):
            decay = decays[k]
            first = k * LANES - strip * STRIP
            local[k] = jnp.sqrt(1.0 - decay * decay) * mixed[:, first : first + LANES]
            state = local[k, strided(0, steps), :]
            factor = decays[k, strided(0, steps), :]
            states, factors = [state], [factor]
            for s in range(1, SUB):
                step_decay = decays[k, strided(s, steps), :]
                state = step_decay * state + local[k, strided(s, steps), :]
                factor = step_decay * factor
                states.append(state)
                factors.append(factor)
            carry = jnp.zeros((1, LANES), jnp.float32)
            entering = []
            for b in range(tiles):
                entering.append(carry)
                carry = factor[b : b + 1, :] * carry + state[b : b + 1, :]
            end_ref[1:2, lanes(k)] = carry
            entering = jnp.concatenate(entering, axis=0)
            for s in range(SUB):
                local[k, strided(s, steps), :] = states[s] + factors[s] * entering
    for reader, (place, rows_ref) in enumerate(((own, own_ref), (near, near_ref), (far, far_ref))):
        for slot in range(capacity):
            _, step, first = tile_at(place, slot, steps, capacity)
            for k in range(FB // LANES):
                rows_ref[slot : slot + 1, lanes(k)] = local[first + k, pl.ds(step, 1), :]
        rows_ref[capacity:, :] = factors_ref[reader * capacity : (reader + 1) * capacity, :]


def piece_row(pieces, per, distance, row):
    found = pieces[0][row : row + 1, :]
    for k, piece in enumerate(pieces[1:]):
        inside = jnp.clip(distance - 2**k, 0, 2**k - 1)
        at = piece[pl.ds(inside * per + row, 1), :]
        found = jnp.where(distance >= 2**k, at, found)
    return found


def observe_kernel(steps, pieces, here, place, block, own_ref, near_ref, far_ref, tiles_ref, *rest):
    ends, (seen_ref, factor_ref, entered, picked) = rest[:pieces], rest[pieces:]
    capacity, soundings, cells = tiles_ref.shape
    windows = 2 ** (pieces - 1)
    width = ends[0].shape[1]
    own = here[0]
    entered[...] = jnp.zeros_like(entered)

    def one(window, state):
        for back in range(BACK + 1):

            @pl.when(window == own - back)
            def _():
                entered[BACK - back : BACK - back + 1, :] = state

        return piece_row(ends, 2, window ^ own, 0) * state + piece_row(ends, 2, window ^ own, 1)

    lax.fori_loop(0, windows, one, jnp.zeros((1, width), jnp.float32), unroll=windows <= 8)
    live = place[2 * capacity]
    for slot in range(capacity):
        which, _, first = tile_at(place, slot, steps, capacity)
        columns = pl.ds(pl.multiple_of(first * LANES, FB), FB)
        row, later = slice(slot, slot + 1), slice(capacity + slot, capacity + slot + 1)
        offset = jnp.where(
            which == 2, own_ref[row, :], jnp.where(which == 1, near_ref[row, :], far_ref[row, :])
        )
        factor = jnp.where(
            which == 2, own_ref[later, :], jnp.where(which == 1, near_ref[later, :], far_ref[later, :])
        )
        factor_ref[row, :] = factor
        value = offset + factor * entered[pl.ds(which, 1), columns]
        picked[row, :] = jnp.where(slot < live, value, 0.0)
    rows = picked[...].astype(jnp.bfloat16)
    products = nt_dot(rows, tiles_ref[...].reshape(capacity * soundings, cells))
    blocks = lax.broadcasted_iota(jnp.int32, seen_ref.shape, 0)
    seen = jnp.zeros(seen_ref.shape, jnp.float32)
    for slot in range(capacity):
        part = products[slot : slot + 1, slot * soundings : (slot + 1) * soundings]
        seen = seen + jnp.where(blocks == block[slot], part, 0.0)
    seen_ref[...] = seen


def adjoint_kernel(
    steps, place, block, seen_ref, other_ref, noise_ref, tiles_ref, factor_ref, rows_ref, sums_ref, weights
):
    capacity, soundings, cells = tiles_ref.shape
    observed = seen_ref[...] + other_ref[...]
    weights[...] = (observed * noise_ref[...]).astype(jnp.bfloat16).astype(jnp.float32)
    slots = lax.broadcasted_iota(jnp.int32, (capacity, soundings), 0)
    live = place[2 * capacity]
    pieces = []
    for slot in range(capacity):
        picked = weights[pl.ds(block[slot], 1), :]
        pieces.append(jnp.where((slots == slot) & (slot < live), picked, 0.0))
    spread = jnp.concatenate(pieces, axis=1).astype(jnp.bfloat16)
    rows = jnp.dot(
        spread,
        tiles_ref[...].reshape(capacity * soundings, cells),
        preferred_element_type=jnp.float32,
    )
    rows_ref[...] = rows
    handed = rows * factor_ref[...]
    sums_ref[...] = jnp.zeros_like(sums_ref)
    for slot in range(capacity):
        which, _, first = tile_at(place, slot, steps, capacity)
        columns = pl.ds(pl.multiple_of(first * LANES, FB), FB)
        at = pl.ds(which, 1)
        sums_ref[at, columns] = sums_ref[at, columns] + handed[slot : slot + 1, :]


def hold_kernel(
    pieces, here, own, near, far, own_ref, near_ref, far_ref, decay_ref, *rest
):
    ends, sums = rest[:pieces], rest[pieces : 2 * pieces]
    pulled_ref, decays, terms = rest[2 * pieces :]
    steps, width = decay_ref.shape
    tiles = steps // SUB
    capacity = own_ref.shape[0]
    windows = 2 ** (pieces - 1)
    me = here[0]
    per = sums[0].shape[0]

    def one(hop, state):
        window = windows - 1 - hop
        arriving = jnp.zeros((1, width), jnp.float32)
        for ahead in range(BACK + 1):
            reader = jnp.minimum(window + ahead, windows - 1)
            arriving = arriving + jnp.where(
                window + ahead < windows, piece_row(sums, per, reader ^ me, BACK - ahead), 0.0
            )
        passed = piece_row(ends, 2, window ^ me, 0) * state + arriving
        return jnp.where(window > me, passed, state)

    incoming = lax.fori_loop(
        0, windows - 1, one, jnp.zeros((1, width), jnp.float32), unroll=windows <= 8
    )
    terms[...] = jnp.zeros_like(terms)
    to_columns(decays, decay_ref[...])
    for reader, (place, rows) in enumerate(((own, own_ref), (near, near_ref), (far, far_ref))):
        live = place[2 * capacity]
        for slot in range(capacity):
            which, step, first = tile_at(place, slot, steps, capacity)
            mine = (which == BACK - reader) & (slot < live)
            step = pl.ds(step, 1)
            for k in range(FB // LANES):
                terms[first + k, step, :] = terms[first + k, step, :] + jnp.where(
                    mine, rows[slot : slot + 1, lanes(k)], 0.0
                )
    for k in range(width // LANES):
        state = terms[k, strided(SUB - 1, steps), :]
        factor = jnp.ones_like(state)
        states, factors = [state], [factor]
        for s in range(SUB - 2, -1, -1):
            step_decay = decays[k, strided(s + 1, steps), :]
            state = terms[k, strided(s, steps), :] + step_decay * state
            factor = step_decay * factor
            states.append(state)
            factors.append(factor)
        first = decays[k, strided(0, steps), :]
        state, factor = first * state, first * factor
        carry = incoming[:, lanes(k)]
        entering = []
        for b in range(tiles - 1, -1, -1):
            entering.insert(0, carry)
            carry = state[b : b + 1, :] + factor[b : b + 1, :] * carry
        entering = jnp.concatenate(entering, axis=0)
        for s in range(SUB):
            terms[k, strided(SUB - 1 - s, steps), :] = states[s] + factors[s] * entering
        decay = decays[k]
        pulled_ref[:, lanes(k)] = (jnp.sqrt(1.0 - decay * decay) * terms[k]).astype(jnp.bfloat16)


def image_kernel(
    region, a_ref, b_ref, spatial, part_ref, direction_ref, residual_ref, image_ref, sums_ref
):
    steps, width = a_ref.shape
    totals = [jnp.zeros((1, STRIP), jnp.float32) for _ in range(4)]
    for strip in range(width // STRIP):
        at = slice(strip * STRIP, (strip + 1) * STRIP)
        direction, residual = direction_ref[:, at], residual_ref[:, at]
        image = direction + (
            part_ref[:, at]
            + product(a_ref, 2, region, spatial, strip)
            + product(b_ref, 3, region, spatial, strip)
        )
        image_ref[:, at] = image
        terms = (residual * residual, direction * image, residual * image, image * image)
        totals = [t + jnp.sum(term, axis=0, keepdims=True) for t, term in zip(totals, terms)]
    sums_ref[...] = jnp.zeros_like(sums_ref)
    for k, total in enumerate(totals):
        sums_ref[k : k + 1, :] = jnp.broadcast_to(
            jnp.sum(total, axis=1, keepdims=True), (1, LANES)
        )


def update_kernel(
    totals_ref, solution_ref, residual_ref, direction_ref, image_ref, solution_new, residual_new, direction_new
):
    norm_old, curvature, cross_sum, image_sq = (totals_ref[k : k + 1, :] for k in range(4))
    step_len = norm_old / curvature
    norm_new = norm_old - 2.0 * step_len * cross_sum + step_len * step_len * image_sq
    ratio = norm_new / norm_old
    for k in range(direction_ref.shape[1] // LANES):
        direction = direction_ref[:, lanes(k)]
        residual = residual_ref[:, lanes(k)] - step_len * image_ref[:, lanes(k)]
        solution_new[:, lanes(k)] = solution_ref[:, lanes(k)] + step_len * direction
        residual_new[:, lanes(k)] = residual
        direction_new[:, lanes(k)] = residual + ratio * direction


def body(
    solution,
    residual,
    direction,
    decay,
    spatial,
    tiles,
    tile_block,
    tile_time,
    tile_cell,
    tile_count,
    noise_inv,
):
    steps, width = direction.shape
    footprint = tiles[0, 0]
    capacity, soundings, cells = footprint.shape
    block_count = noise_inv.shape[0]
    here = lax.axis_index("tm").astype(jnp.int32).reshape(1)
    region = lax.axis_index("region").astype(jnp.int32).reshape(1)
    block = tile_block[0, 0]
    place = jnp.concatenate([tile_time[0, 0], tile_cell[0, 0], tile_count[0]])
    f32 = jnp.float32
    columns = pltpu.VMEM((width // LANES, steps, LANES), f32)

    blocks = region_blocks(direction.astype(jnp.bfloat16))
    near, far = (shifted(place, "tm", -hop) for hop in range(1, BACK + 1))
    places = [place, near, far]
    factors, last = on_chip(
        decay_kernel,
        places,
        [decay],
        [(((BACK + 1) * capacity, cells), f32), ((1, width), f32)],
        [columns, pltpu.VMEM((width // LANES, steps // SUB, LANES), f32)],
        "decay_rows",
    )
    (part,) = on_chip(
        first_kernel,
        [region],
        [blocks[0], blocks[1], spatial],
        [((steps, width), f32)],
        name="first_products",
    )
    own_rows, near_rows, far_rows, end = on_chip(
        filter_kernel,
        [region] + places,
        [blocks[2], blocks[3], spatial, part, decay, factors, last],
        [((2 * capacity, cells), f32)] * (BACK + 1) + [((2, width), f32)],
        [columns, columns],
        "filter_rows",
    )
    near_rows, far_rows = shifted(near_rows, "tm", 1), shifted(far_rows, "tm", 2)
    ends = window_rows(end)
    seen, factors = on_chip(
        lambda *refs: observe_kernel(steps, len(ends), *refs),
        [here, place, block],
        [own_rows, near_rows, far_rows, footprint] + ends,
        [((block_count, soundings), f32), ((capacity, cells), f32)],
        [pltpu.VMEM((SUB, width), f32), pltpu.VMEM((capacity, cells), f32)],
        "observe",
    )
    bit = 1
    while bit < lax.axis_size("region") // 2:
        seen = seen + swapped(seen, "region", bit)
        bit *= 2
    rows, sums = on_chip(
        lambda *refs: adjoint_kernel(steps, *refs),
        [place, block],
        [seen, swapped(seen, "region", bit), noise_inv, footprint, factors],
        [((capacity, cells), f32), ((BACK + 2, width), f32)],
        [pltpu.VMEM(noise_inv.shape, f32)],
        "adjoint_rows",
    )
    near_rows, far_rows = (shifted(rows, "tm", -hop) for hop in range(1, BACK + 1))
    (pulled,) = on_chip(
        lambda *refs: hold_kernel(len(ends), *refs),
        [here] + places,
        [rows, near_rows, far_rows, decay] + ends + window_rows(sums),
        [((steps, width), jnp.bfloat16)],
        [columns, columns],
        "hold",
    )
    blocks = region_blocks(pulled)
    (part,) = on_chip(
        first_kernel,
        [region],
        [blocks[0], blocks[1], spatial],
        [((steps, width), f32)],
        name="first_products",
    )
    image, totals = on_chip(
        image_kernel,
        [region],
        [blocks[2], blocks[3], spatial, part, direction, residual],
        [((steps, width), f32), ((SUB, LANES), f32)],
        name="make_image",
    )
    for axis in ("region", "tm"):
        bit = 1
        while bit < lax.axis_size(axis):
            totals = totals + swapped(totals, axis, bit)
            bit *= 2
    return on_chip(
        update_kernel,
        [],
        [totals, solution, residual, direction, image],
        [((steps, width), f32)] * 3,
        name="update",
        out_spaces=[jax.ShapeDtypeStruct] * 3,
    )


def solution(mesh):
    return jax.shard_map(
        body,
        mesh=mesh,
        in_specs=(
            P("tm", "region"),
            P("tm", "region"),
            P("tm", "region"),
            P("tm", "region"),
            P("region", None),
            P("tm", "region", None, None, None),
            P("tm", "region", None),
            P("tm", "region", None),
            P("tm", "region", None),
            P("tm", "region"),
            P("tm", None),
        ),
        out_specs=(P("tm", "region"), P("tm", "region"), P("tm", "region")),
        check_vma=False,
    )
```

```python
import jax
import jax.numpy as jnp
from jax import lax
from jax.experimental import pallas as pl
from jax.experimental.pallas import tpu as pltpu
from jax.sharding import PartitionSpec as P


FB = 512
BACK = 2
STRIP = 256
SUB = 8
LANES = 128
KERNEL_VMEM = 12 * 2**20


def swapped(block, axis, bit):
    return lax.ppermute(block, axis, [(i, i ^ bit) for i in range(lax.axis_size(axis))])


def shifted(block, axis, distance):
    devices = range(lax.axis_size(axis))
    route = [(i - distance, i) for i in devices if i - distance in devices]
    return lax.ppermute(block, axis, route)


def region_blocks(block):
    blocks, bit = {0: block}, lax.axis_size("region") // 2
    while bit:
        blocks.update({k ^ bit: swapped(b, "region", bit) for k, b in list(blocks.items())})
        bit //= 2
    return blocks


def window_rows(rows):
    bit, pieces = 1, [rows]
    while bit < lax.axis_size("tm"):
        joined = jnp.concatenate(pieces, axis=0) if len(pieces) > 1 else rows
        pieces.append(swapped(joined, "tm", bit))
        bit *= 2
    return pieces


def nt_dot(a, b):
    return lax.dot_general(a, b, (((1,), (1,)), ((), ())), preferred_element_type=jnp.float32)


def strided(start, steps):
    return pl.ds(start, steps // SUB, stride=SUB)


def lanes(k):
    return slice(k * LANES, (k + 1) * LANES)


def on_chip(kernel, scalars, arrays, outs, scratch=(), out_spaces=None, outside=()):
    spaces = out_spaces or [pltpu.VMEM] * len(outs)
    call = pl.pallas_call(
        kernel,
        out_shape=tuple(space(shape, dtype) for space, (shape, dtype) in zip(spaces, outs)),
        in_specs=[pl.BlockSpec(memory_space=pltpu.SMEM)] * len(scalars)
        + [pl.BlockSpec(memory_space=pltpu.VMEM)] * len(arrays)
        + [pl.BlockSpec(memory_space=pl.ANY)] * len(outside),
        out_specs=tuple(pl.BlockSpec(memory_space=pltpu.VMEM) for _ in outs),
        scratch_shapes=list(scratch),
        compiler_params=pltpu.CompilerParams(vmem_limit_bytes=KERNEL_VMEM),
    )
    arrays = [pltpu.with_memory_space_constraint(a, pltpu.VMEM) for a in arrays]
    return call(
        *scalars,
        *arrays,
        *(pltpu.with_memory_space_constraint(a, pltpu.HBM) for a in outside),
    )


def slots_of(place):
    return (place.shape[0] - 1) // 3


def tile_at(place, slot, steps):
    time = place[slot]
    return time // steps, time % steps, place[slots_of(place) + slot] * (FB // LANES)


def product(block, place, region, spatial, strip):
    width = block.shape[1]
    columns = pl.ds(pl.multiple_of((region[0] ^ place) * width, width), width)
    return nt_dot(block[...], spatial[strip * STRIP : (strip + 1) * STRIP, columns])


def first_kernel(region, a_ref, b_ref, spatial, out_ref):
    for strip in range(out_ref.shape[1] // STRIP):
        out_ref[:, strip * STRIP : (strip + 1) * STRIP] = product(
            a_ref, 0, region, spatial, strip
        ) + product(b_ref, 1, region, spatial, strip)


def fetch(region, spatial_hbm, spatial, arrived):
    width = spatial.shape[1] // arrived.shape[0]
    copies = []
    for place in range(arrived.shape[0]):
        columns = pl.ds(pl.multiple_of((region[0] ^ place) * width, width), width)
        copies.append(
            pltpu.make_async_copy(
                spatial_hbm.at[:, columns], spatial.at[:, columns], arrived.at[place]
            )
        )
        copies[-1].start()
    return copies


def fetch_kernel(region, a_ref, b_ref, spatial_hbm, part_ref, spatial, arrived):
    copies = fetch(region, spatial_hbm, spatial, arrived)
    copies[0].wait()
    copies[1].wait()
    first_kernel(region, a_ref, b_ref, spatial, part_ref)
    for copy in copies[2:]:
        copy.wait()


def second_kernel(region, a_ref, spatial, part_ref, out_ref):
    for strip in range(out_ref.shape[1] // STRIP):
        at = slice(strip * STRIP, (strip + 1) * STRIP)
        out_ref[:, at] = part_ref[:, at] + product(a_ref, 2, region, spatial, strip)


def prepare_kernel(
    region,
    a_ref,
    b_ref,
    decay_hbm,
    spatial_hbm,
    part_ref,
    prefix_ref,
    decays_ref,
    gains_ref,
    last_ref,
    spatial,
    arrived,
    decay_arrived,
):
    steps, width = a_ref.shape
    tiles = steps // SUB
    decay_copies = []
    for k in range(width // LANES):
        decay_copies.append(
            pltpu.make_async_copy(
                decay_hbm.at[:, pl.ds(k * LANES, LANES)], decays_ref.at[k], decay_arrived.at[k]
            )
        )
        decay_copies[-1].start()
    copies = fetch(region, spatial_hbm, spatial, arrived)
    for k in range(width // LANES):
        decay_copies[k].wait()
        decay = decays_ref[k]
        gains_ref[k] = jnp.sqrt(1.0 - decay * decay)
        running = [decays_ref[k, strided(0, steps), :]]
        for s in range(1, SUB):
            running.append(running[-1] * decays_ref[k, strided(s, steps), :])
        state = jnp.ones((1, LANES), jnp.float32)
        carried = []
        for b in range(tiles):
            carried.append(state)
            state = state * running[-1][b : b + 1, :]
        last_ref[:, lanes(k)] = state
        carried = jnp.concatenate(carried, axis=0)
        for s in range(SUB):
            prefix_ref[k, strided(s, steps), :] = running[s] * carried
    copies[0].wait()
    copies[1].wait()
    first_kernel(region, a_ref, b_ref, spatial, part_ref)
    for copy in copies[2:]:
        copy.wait()


def filter_kernel(
    region, b_ref, spatial, part_ref, decays, gains, last_ref, local, end_ref
):
    steps, width = b_ref.shape
    tiles = steps // SUB
    end_ref[0:1, :] = last_ref[...]
    for strip in range(width // STRIP):
        mixed = part_ref[:, strip * STRIP : (strip + 1) * STRIP] + product(
            b_ref, 3, region, spatial, strip
        )
        for k in range(strip * STRIP // LANES, (strip + 1) * STRIP // LANES):
            first = k * LANES - strip * STRIP
            local[k] = gains[k] * mixed[:, first : first + LANES]
            state = local[k, strided(0, steps), :]
            factor = decays[k, strided(0, steps), :]
            states, factors = [state], [factor]
            for s in range(1, SUB):
                step_decay = decays[k, strided(s, steps), :]
                state = step_decay * state + local[k, strided(s, steps), :]
                factor = step_decay * factor
                states.append(state)
                factors.append(factor)
            carry = jnp.zeros((1, LANES), jnp.float32)
            entering = []
            for b in range(tiles):
                entering.append(carry)
                carry = factor[b : b + 1, :] * carry + state[b : b + 1, :]
            end_ref[1:2, lanes(k)] = carry
            entering = jnp.concatenate(entering, axis=0)
            for s in range(SUB):
                local[k, strided(s, steps), :] = states[s] + factors[s] * entering


def gather_kernel(own, near, far, local, prefix_ref, own_ref, near_ref, far_ref):
    steps = local.shape[1]
    capacity = own_ref.shape[0] // 2
    for place, rows_ref in ((own, own_ref), (near, near_ref), (far, far_ref)):
        for slot in range(capacity):
            _, step, first = tile_at(place, slot, steps)
            for k in range(FB // LANES):
                at = (first + k, pl.ds(step, 1))
                rows_ref[slot : slot + 1, lanes(k)] = local[*at, :]
                rows_ref[capacity + slot : capacity + slot + 1, lanes(k)] = prefix_ref[*at, :]


def piece_row(pieces, per, distance, row):
    found = pieces[0][row : row + 1, :]
    for k, piece in enumerate(pieces[1:]):
        inside = jnp.clip(distance - 2**k, 0, 2**k - 1)
        at = piece[pl.ds(inside * per + row, 1), :]
        found = jnp.where(distance >= 2**k, at, found)
    return found


def observe_kernel(steps, pieces, here, place, own_ref, near_ref, far_ref, tiles_ref, *rest):
    ends, (seen_ref, factor_ref, entered, picked) = rest[:pieces], rest[pieces:]
    capacity, soundings, cells = tiles_ref.shape
    windows = 2 ** (pieces - 1)
    width = ends[0].shape[1]
    own = here[0]
    entered[...] = jnp.zeros_like(entered)

    def one(window, state):
        for back in range(BACK + 1):

            @pl.when(window == own - back)
            def _():
                entered[BACK - back : BACK - back + 1, :] = state

        return piece_row(ends, 2, window ^ own, 0) * state + piece_row(ends, 2, window ^ own, 1)

    lax.fori_loop(0, windows, one, jnp.zeros((1, width), jnp.float32), unroll=windows <= 8)
    live = place[3 * capacity]
    for slot in range(capacity):
        which, _, first = tile_at(place, slot, steps)
        columns = pl.ds(pl.multiple_of(first * LANES, FB), FB)
        row, later = slice(slot, slot + 1), slice(capacity + slot, capacity + slot + 1)
        offset = jnp.where(
            which == 2, own_ref[row, :], jnp.where(which == 1, near_ref[row, :], far_ref[row, :])
        )
        factor = jnp.where(
            which == 2, own_ref[later, :], jnp.where(which == 1, near_ref[later, :], far_ref[later, :])
        )
        factor_ref[row, :] = factor
        value = offset + factor * entered[pl.ds(which, 1), columns]
        picked[row, :] = jnp.where(slot < live, value, 0.0)
    rows = picked[...].astype(jnp.bfloat16)
    products = nt_dot(rows, tiles_ref[...].reshape(capacity * soundings, cells))
    blocks = lax.broadcasted_iota(jnp.int32, seen_ref.shape, 0)
    seen = jnp.zeros(seen_ref.shape, jnp.float32)
    for slot in range(capacity):
        part = products[slot : slot + 1, slot * soundings : (slot + 1) * soundings]
        seen = seen + jnp.where(blocks == place[2 * capacity + slot], part, 0.0)
    seen_ref[...] = seen


def adjoint_kernel(
    steps, place, seen_ref, other_ref, noise_ref, tiles_ref, factor_ref, rows_ref, sums_ref, weights
):
    capacity, soundings, cells = tiles_ref.shape
    observed = seen_ref[...] + other_ref[...]
    weights[...] = (observed * noise_ref[...]).astype(jnp.bfloat16).astype(jnp.float32)
    slots = lax.broadcasted_iota(jnp.int32, (capacity, soundings), 0)
    live = place[3 * capacity]
    pieces = []
    for slot in range(capacity):
        picked = weights[pl.ds(place[2 * capacity + slot], 1), :]
        pieces.append(jnp.where((slots == slot) & (slot < live), picked, 0.0))
    spread = jnp.concatenate(pieces, axis=1).astype(jnp.bfloat16)
    rows = jnp.dot(
        spread,
        tiles_ref[...].reshape(capacity * soundings, cells),
        preferred_element_type=jnp.float32,
    )
    rows_ref[...] = rows
    handed = rows * factor_ref[...]
    sums_ref[...] = jnp.zeros_like(sums_ref)
    for slot in range(capacity):
        which, _, first = tile_at(place, slot, steps)
        columns = pl.ds(pl.multiple_of(first * LANES, FB), FB)
        at = pl.ds(which, 1)
        sums_ref[at, columns] = sums_ref[at, columns] + handed[slot : slot + 1, :]


def hold_kernel(
    pieces, here, own, near, far, own_ref, near_ref, far_ref, decays, gains, *rest
):
    ends, sums = rest[:pieces], rest[pieces : 2 * pieces]
    pulled_ref, terms = rest[2 * pieces :]
    steps, width = pulled_ref.shape
    tiles = steps // SUB
    capacity = own_ref.shape[0]
    windows = 2 ** (pieces - 1)
    me = here[0]
    per = sums[0].shape[0]

    def one(hop, state):
        window = windows - 1 - hop
        arriving = jnp.zeros((1, width), jnp.float32)
        for ahead in range(BACK + 1):
            reader = jnp.minimum(window + ahead, windows - 1)
            arriving = arriving + jnp.where(
                window + ahead < windows, piece_row(sums, per, reader ^ me, BACK - ahead), 0.0
            )
        passed = piece_row(ends, 2, window ^ me, 0) * state + arriving
        return jnp.where(window > me, passed, state)

    incoming = lax.fori_loop(
        0, windows - 1, one, jnp.zeros((1, width), jnp.float32), unroll=windows <= 8
    )
    terms[...] = jnp.zeros_like(terms)
    for reader, (place, rows) in enumerate(((own, own_ref), (near, near_ref), (far, far_ref))):
        live = place[3 * capacity]
        for slot in range(capacity):
            which, step, first = tile_at(place, slot, steps)
            mine = (which == BACK - reader) & (slot < live)
            step = pl.ds(step, 1)
            for k in range(FB // LANES):
                terms[first + k, step, :] = terms[first + k, step, :] + jnp.where(
                    mine, rows[slot : slot + 1, lanes(k)], 0.0
                )
    for k in range(width // LANES):
        state = terms[k, strided(SUB - 1, steps), :]
        factor = jnp.ones_like(state)
        states, factors = [state], [factor]
        for s in range(SUB - 2, -1, -1):
            step_decay = decays[k, strided(s + 1, steps), :]
            state = terms[k, strided(s, steps), :] + step_decay * state
            factor = step_decay * factor
            states.append(state)
            factors.append(factor)
        first = decays[k, strided(0, steps), :]
        state, factor = first * state, first * factor
        carry = incoming[:, lanes(k)]
        entering = []
        for b in range(tiles - 1, -1, -1):
            entering.insert(0, carry)
            carry = state[b : b + 1, :] + factor[b : b + 1, :] * carry
        entering = jnp.concatenate(entering, axis=0)
        for s in range(SUB):
            terms[k, strided(SUB - 1 - s, steps), :] = states[s] + factors[s] * entering
        pulled_ref[:, lanes(k)] = (gains[k] * terms[k]).astype(jnp.bfloat16)


def image_kernel(
    region, b_ref, spatial, part_ref, direction_ref, residual_ref, image_ref, sums_ref
):
    _, width = b_ref.shape
    totals = [jnp.zeros((1, STRIP), jnp.float32) for _ in range(4)]
    for strip in range(width // STRIP):
        at = slice(strip * STRIP, (strip + 1) * STRIP)
        direction, residual = direction_ref[:, at], residual_ref[:, at]
        image = direction + (part_ref[:, at] + product(b_ref, 3, region, spatial, strip))
        image_ref[:, at] = image
        terms = (residual * residual, direction * image, residual * image, image * image)
        totals = [t + jnp.sum(term, axis=0, keepdims=True) for t, term in zip(totals, terms)]
    sums_ref[...] = jnp.zeros_like(sums_ref)
    for k, total in enumerate(totals):
        sums_ref[k : k + 1, :] = jnp.broadcast_to(
            jnp.sum(total, axis=1, keepdims=True), (1, LANES)
        )


def update_kernel(
    totals_ref, solution_ref, residual_ref, direction_ref, image_ref, solution_new, residual_new, direction_new
):
    norm_old, curvature, cross_sum, image_sq = (totals_ref[k : k + 1, :] for k in range(4))
    step_len = norm_old / curvature
    norm_new = norm_old - 2.0 * step_len * cross_sum + step_len * step_len * image_sq
    ratio = norm_new / norm_old
    for k in range(direction_ref.shape[1] // LANES):
        direction = direction_ref[:, lanes(k)]
        residual = residual_ref[:, lanes(k)] - step_len * image_ref[:, lanes(k)]
        solution_new[:, lanes(k)] = solution_ref[:, lanes(k)] + step_len * direction
        residual_new[:, lanes(k)] = residual
        direction_new[:, lanes(k)] = residual + ratio * direction


def body(
    solution,
    residual,
    direction,
    decay,
    spatial,
    tiles,
    tile_block,
    tile_time,
    tile_cell,
    tile_count,
    noise_inv,
):
    steps, width = direction.shape
    footprint = tiles[0, 0]
    capacity, soundings, cells = footprint.shape
    block_count = noise_inv.shape[0]
    here = lax.axis_index("tm").astype(jnp.int32).reshape(1)
    region = lax.axis_index("region").astype(jnp.int32).reshape(1)
    f32 = jnp.float32
    columns = pltpu.VMEM((width // LANES, steps, LANES), f32)
    regions = spatial.shape[1] // width

    place = jnp.concatenate([tile_time[0, 0], tile_cell[0, 0], tile_block[0, 0], tile_count[0]])
    half = direction.astype(jnp.bfloat16)
    blocks = region_blocks(half)
    part, prefix, decays, gains, last, kept = on_chip(
        prepare_kernel,
        [region],
        [blocks[0], blocks[1]],
        [((steps, width), f32)]
        + [(columns.shape, f32)] * 3
        + [((1, width), f32), (spatial.shape, spatial.dtype)],
        [pltpu.SemaphoreType.DMA((regions,)), pltpu.SemaphoreType.DMA((width // LANES,))],
        outside=[decay, spatial],
    )
    (part,) = on_chip(second_kernel, [region], [blocks[2], kept, part], [((steps, width), f32)])
    places = [place, shifted(place, "tm", -1), shifted(place, "tm", -2)]
    local, end = on_chip(
        filter_kernel,
        [region],
        [blocks[3], kept, part, decays, gains, last],
        [(columns.shape, f32), ((2, width), f32)],
    )
    own_rows, near_rows, far_rows = on_chip(
        gather_kernel, places, [local, prefix], [((2 * capacity, cells), f32)] * (BACK + 1)
    )
    near_rows = shifted(near_rows, "tm", 1)
    far_rows = shifted(far_rows, "tm", 2)
    ends = window_rows(end)
    seen, factors = on_chip(
        lambda *refs: observe_kernel(steps, len(ends), *refs),
        [here, place],
        [own_rows, near_rows, far_rows, footprint] + ends,
        [((block_count, soundings), f32), ((capacity, cells), f32)],
        [pltpu.VMEM((SUB, width), f32), pltpu.VMEM((capacity, cells), f32)],
    )
    bit = 1
    while bit < lax.axis_size("region") // 2:
        seen = seen + swapped(seen, "region", bit)
        bit *= 2
    rows, sums = on_chip(
        lambda *refs: adjoint_kernel(steps, *refs),
        [place],
        [seen, swapped(seen, "region", bit), noise_inv, footprint, factors],
        [((capacity, cells), f32), ((BACK + 2, width), f32)],
        [pltpu.VMEM(noise_inv.shape, f32)],
    )
    near_rows = shifted(rows, "tm", -1)
    far_rows = shifted(rows, "tm", -2)
    (pulled,) = on_chip(
        lambda *refs: hold_kernel(len(ends), *refs),
        [here] + places,
        [rows, near_rows, far_rows, decays, gains] + ends + window_rows(sums),
        [((steps, width), jnp.bfloat16)],
        [columns],
    )
    blocks = region_blocks(pulled)
    part, kept = on_chip(
        fetch_kernel,
        [region],
        [blocks[0], blocks[1]],
        [((steps, width), f32), (spatial.shape, spatial.dtype)],
        [pltpu.SemaphoreType.DMA((regions,))],
        outside=[spatial],
    )
    (part,) = on_chip(second_kernel, [region], [blocks[2], kept, part], [((steps, width), f32)])
    image, totals = on_chip(
        image_kernel,
        [region],
        [blocks[3], kept, part, direction, residual],
        [((steps, width), f32), ((SUB, LANES), f32)],
    )
    for axis in ("region", "tm"):
        bit = 1
        while bit < lax.axis_size(axis):
            totals = totals + swapped(totals, axis, bit)
            bit *= 2
    return on_chip(
        update_kernel,
        [],
        [totals, solution, residual, direction, image],
        [((steps, width), f32)] * 3,
        out_spaces=[jax.ShapeDtypeStruct] * 3,
    )


def solution(mesh):
    return jax.shard_map(
        body,
        mesh=mesh,
        in_specs=(
            P("tm", "region"),
            P("tm", "region"),
            P("tm", "region"),
            P("tm", "region"),
            P("region", None),
            P("tm", "region", None, None, None),
            P("tm", "region", None),
            P("tm", "region", None),
            P("tm", "region", None),
            P("tm", "region"),
            P("tm", None),
        ),
        out_specs=(P("tm", "region"), P("tm", "region"), P("tm", "region")),
        check_vma=False,
    )
```

```python
import jax
import jax.numpy as jnp
from jax import lax
from jax.experimental import pallas as pl
from jax.experimental.pallas import tpu as pltpu
from jax.sharding import PartitionSpec as P


FB = 512
BACK = 2
STRIP = 256
SUB = 8
LANES = 128
KERNEL_VMEM = 12 * 2**20


def swapped(block, axis, bit):
    return lax.ppermute(block, axis, [(i, i ^ bit) for i in range(lax.axis_size(axis))])


def shifted(block, axis, distance):
    devices = range(lax.axis_size(axis))
    route = [(i - distance, i) for i in devices if i - distance in devices]
    return lax.ppermute(block, axis, route)


def region_blocks(block):
    blocks, bit = {0: block}, lax.axis_size("region") // 2
    while bit:
        blocks.update({k ^ bit: swapped(b, "region", bit) for k, b in list(blocks.items())})
        bit //= 2
    return blocks


def window_rows(rows):
    bit, pieces = 1, [rows]
    while bit < lax.axis_size("tm"):
        joined = jnp.concatenate(pieces, axis=0) if len(pieces) > 1 else rows
        pieces.append(swapped(joined, "tm", bit))
        bit *= 2
    return pieces


def nt_dot(a, b):
    return lax.dot_general(a, b, (((1,), (1,)), ((), ())), preferred_element_type=jnp.float32)


def strided(start, steps):
    return pl.ds(start, steps // SUB, stride=SUB)


def lanes(k):
    return slice(k * LANES, (k + 1) * LANES)


def on_chip(kernel, scalars, arrays, outs, scratch=(), out_spaces=None, outside=()):
    spaces = out_spaces or [pltpu.VMEM] * len(outs)
    call = pl.pallas_call(
        kernel,
        out_shape=tuple(space(shape, dtype) for space, (shape, dtype) in zip(spaces, outs)),
        in_specs=[pl.BlockSpec(memory_space=pltpu.SMEM)] * len(scalars)
        + [pl.BlockSpec(memory_space=pltpu.VMEM)] * len(arrays)
        + [pl.BlockSpec(memory_space=pl.ANY)] * len(outside),
        out_specs=tuple(pl.BlockSpec(memory_space=pltpu.VMEM) for _ in outs),
        scratch_shapes=list(scratch),
        compiler_params=pltpu.CompilerParams(vmem_limit_bytes=KERNEL_VMEM),
    )
    arrays = [pltpu.with_memory_space_constraint(a, pltpu.VMEM) for a in arrays]
    return call(
        *scalars,
        *arrays,
        *(pltpu.with_memory_space_constraint(a, pltpu.HBM) for a in outside),
    )


def slots_of(place):
    return place.shape[0] // 4


def tile_at(place, slot, steps):
    time = place[slot]
    return time // steps, time % steps, place[slots_of(place) + slot] * (FB // LANES)


def product(block, place, region, spatial, strip):
    width = block.shape[1]
    columns = pl.ds(pl.multiple_of((region[0] ^ place) * width, width), width)
    return nt_dot(block[...], spatial[strip * STRIP : (strip + 1) * STRIP, columns])


def first_kernel(region, a_ref, b_ref, spatial, out_ref):
    for strip in range(out_ref.shape[1] // STRIP):
        out_ref[:, strip * STRIP : (strip + 1) * STRIP] = product(
            a_ref, 0, region, spatial, strip
        ) + product(b_ref, 1, region, spatial, strip)


def fetch(region, spatial_hbm, spatial, arrived):
    width = spatial.shape[1] // arrived.shape[0]
    copies = []
    for place in range(arrived.shape[0]):
        columns = pl.ds(pl.multiple_of((region[0] ^ place) * width, width), width)
        copies.append(
            pltpu.make_async_copy(
                spatial_hbm.at[:, columns], spatial.at[:, columns], arrived.at[place]
            )
        )
        copies[-1].start()
    return copies


def fetch_kernel(region, a_ref, b_ref, spatial_hbm, part_ref, spatial, arrived):
    copies = fetch(region, spatial_hbm, spatial, arrived)
    copies[0].wait()
    copies[1].wait()
    first_kernel(region, a_ref, b_ref, spatial, part_ref)
    for copy in copies[2:]:
        copy.wait()


def second_kernel(region, a_ref, spatial, part_ref, out_ref):
    for strip in range(out_ref.shape[1] // STRIP):
        at = slice(strip * STRIP, (strip + 1) * STRIP)
        out_ref[:, at] = part_ref[:, at] + product(a_ref, 2, region, spatial, strip)


def prepare_kernel(
    region,
    a_ref,
    b_ref,
    decay_hbm,
    spatial_hbm,
    part_ref,
    prefix_ref,
    decays_ref,
    gains_ref,
    last_ref,
    spatial,
    arrived,
    decay_arrived,
):
    steps, width = a_ref.shape
    tiles = steps // SUB
    decay_copies = []
    for k in range(width // LANES):
        decay_copies.append(
            pltpu.make_async_copy(
                decay_hbm.at[:, pl.ds(k * LANES, LANES)], decays_ref.at[k], decay_arrived.at[k]
            )
        )
        decay_copies[-1].start()
    copies = fetch(region, spatial_hbm, spatial, arrived)
    for k in range(width // LANES):
        decay_copies[k].wait()
        decay = decays_ref[k]
        gains_ref[k] = jnp.sqrt(1.0 - decay * decay)
        running = [decays_ref[k, strided(0, steps), :]]
        for s in range(1, SUB):
            running.append(running[-1] * decays_ref[k, strided(s, steps), :])
        state = jnp.ones((1, LANES), jnp.float32)
        carried = []
        for b in range(tiles):
            carried.append(state)
            state = state * running[-1][b : b + 1, :]
        last_ref[:, lanes(k)] = state
        carried = jnp.concatenate(carried, axis=0)
        for s in range(SUB):
            prefix_ref[k, strided(s, steps), :] = running[s] * carried
    copies[0].wait()
    copies[1].wait()
    first_kernel(region, a_ref, b_ref, spatial, part_ref)
    for copy in copies[2:]:
        copy.wait()


def filter_kernel(
    region, b_ref, spatial, part_ref, decays, gains, last_ref, local, end_ref
):
    steps, width = b_ref.shape
    tiles = steps // SUB
    end_ref[0:1, :] = last_ref[...]
    for strip in range(width // STRIP):
        mixed = part_ref[:, strip * STRIP : (strip + 1) * STRIP] + product(
            b_ref, 3, region, spatial, strip
        )
        for k in range(strip * STRIP // LANES, (strip + 1) * STRIP // LANES):
            first = k * LANES - strip * STRIP
            local[k] = gains[k] * mixed[:, first : first + LANES]
            state = local[k, strided(0, steps), :]
            factor = decays[k, strided(0, steps), :]
            states, factors = [state], [factor]
            for s in range(1, SUB):
                step_decay = decays[k, strided(s, steps), :]
                state = step_decay * state + local[k, strided(s, steps), :]
                factor = step_decay * factor
                states.append(state)
                factors.append(factor)
            carry = jnp.zeros((1, LANES), jnp.float32)
            entering = []
            for b in range(tiles):
                entering.append(carry)
                carry = factor[b : b + 1, :] * carry + state[b : b + 1, :]
            end_ref[1:2, lanes(k)] = carry
            entering = jnp.concatenate(entering, axis=0)
            for s in range(SUB):
                local[k, strided(s, steps), :] = states[s] + factors[s] * entering


def gather_kernel(own, near, far, local, prefix_ref, own_ref, near_ref, far_ref):
    steps = local.shape[1]
    capacity = own_ref.shape[0] // 2
    for place, rows_ref in ((own, own_ref), (near, near_ref), (far, far_ref)):
        for slot in range(capacity):
            _, step, first = tile_at(place, slot, steps)
            for k in range(FB // LANES):
                at = (first + k, pl.ds(step, 1))
                rows_ref[slot : slot + 1, lanes(k)] = local[*at, :]
                rows_ref[capacity + slot : capacity + slot + 1, lanes(k)] = prefix_ref[*at, :]


def piece_row(pieces, per, distance, row):
    found = pieces[0][row : row + 1, :]
    for k, piece in enumerate(pieces[1:]):
        inside = jnp.clip(distance - 2**k, 0, 2**k - 1)
        at = piece[pl.ds(inside * per + row, 1), :]
        found = jnp.where(distance >= 2**k, at, found)
    return found


def observe_kernel(steps, pieces, here, place, own_ref, near_ref, far_ref, tiles_ref, *rest):
    ends, (seen_ref, factor_ref, entered, picked) = rest[:pieces], rest[pieces:]
    capacity, soundings, cells = tiles_ref.shape
    windows = 2 ** (pieces - 1)
    width = ends[0].shape[1]
    own = here[0]
    entered[...] = jnp.zeros_like(entered)

    def one(window, state):
        for back in range(BACK + 1):

            @pl.when(window == own - back)
            def _():
                entered[BACK - back : BACK - back + 1, :] = state

        return piece_row(ends, 2, window ^ own, 0) * state + piece_row(ends, 2, window ^ own, 1)

    lax.fori_loop(0, windows, one, jnp.zeros((1, width), jnp.float32), unroll=windows <= 8)
    for slot in range(capacity):
        which, _, first = tile_at(place, slot, steps)
        columns = pl.ds(pl.multiple_of(first * LANES, FB), FB)
        row, later = slice(slot, slot + 1), slice(capacity + slot, capacity + slot + 1)
        offset = jnp.where(
            which == 2, own_ref[row, :], jnp.where(which == 1, near_ref[row, :], far_ref[row, :])
        )
        factor = jnp.where(
            which == 2, own_ref[later, :], jnp.where(which == 1, near_ref[later, :], far_ref[later, :])
        )
        factor_ref[row, :] = factor
        value = offset + factor * entered[pl.ds(which, 1), columns]
        picked[row, :] = jnp.where(place[3 * capacity + slot] == 1, value, 0.0)
    rows = picked[...].astype(jnp.bfloat16)
    products = nt_dot(rows, tiles_ref[...].reshape(capacity * soundings, cells))
    blocks = lax.broadcasted_iota(jnp.int32, seen_ref.shape, 0)
    seen = jnp.zeros(seen_ref.shape, jnp.float32)
    for slot in range(capacity):
        part = products[slot : slot + 1, slot * soundings : (slot + 1) * soundings]
        seen = seen + jnp.where(blocks == place[2 * capacity + slot], part, 0.0)
    seen_ref[...] = seen


def adjoint_kernel(
    steps, place, seen_ref, other_ref, noise_ref, tiles_ref, factor_ref, rows_ref, sums_ref, weights
):
    capacity, soundings, cells = tiles_ref.shape
    observed = seen_ref[...] + other_ref[...]
    weights[...] = (observed * noise_ref[...]).astype(jnp.bfloat16).astype(jnp.float32)
    slots = lax.broadcasted_iota(jnp.int32, (capacity, soundings), 0)
    pieces = []
    for slot in range(capacity):
        picked = weights[pl.ds(place[2 * capacity + slot], 1), :]
        pieces.append(jnp.where((slots == slot) & (place[3 * capacity + slot] == 1), picked, 0.0))
    spread = jnp.concatenate(pieces, axis=1).astype(jnp.bfloat16)
    rows = jnp.dot(
        spread,
        tiles_ref[...].reshape(capacity * soundings, cells),
        preferred_element_type=jnp.float32,
    )
    rows_ref[...] = rows
    handed = rows * factor_ref[...]
    sums_ref[...] = jnp.zeros_like(sums_ref)
    for slot in range(capacity):
        which, _, first = tile_at(place, slot, steps)
        columns = pl.ds(pl.multiple_of(first * LANES, FB), FB)
        at = pl.ds(which, 1)
        sums_ref[at, columns] = sums_ref[at, columns] + handed[slot : slot + 1, :]


def hold_kernel(
    pieces, here, own, near, far, own_ref, near_ref, far_ref, decays, gains, *rest
):
    ends, sums = rest[:pieces], rest[pieces : 2 * pieces]
    pulled_ref, terms = rest[2 * pieces :]
    steps, width = pulled_ref.shape
    tiles = steps // SUB
    capacity = own_ref.shape[0]
    windows = 2 ** (pieces - 1)
    me = here[0]
    per = sums[0].shape[0]

    def one(hop, state):
        window = windows - 1 - hop
        arriving = jnp.zeros((1, width), jnp.float32)
        for ahead in range(BACK + 1):
            reader = jnp.minimum(window + ahead, windows - 1)
            arriving = arriving + jnp.where(
                window + ahead < windows, piece_row(sums, per, reader ^ me, BACK - ahead), 0.0
            )
        passed = piece_row(ends, 2, window ^ me, 0) * state + arriving
        return jnp.where(window > me, passed, state)

    incoming = lax.fori_loop(
        0, windows - 1, one, jnp.zeros((1, width), jnp.float32), unroll=windows <= 8
    )
    terms[...] = jnp.zeros_like(terms)
    for reader, (place, rows) in enumerate(((own, own_ref), (near, near_ref), (far, far_ref))):
        for slot in range(capacity):
            which, step, first = tile_at(place, slot, steps)
            mine = (which == BACK - reader) & (place[3 * capacity + slot] == 1)
            step = pl.ds(step, 1)
            for k in range(FB // LANES):
                terms[first + k, step, :] = terms[first + k, step, :] + jnp.where(
                    mine, rows[slot : slot + 1, lanes(k)], 0.0
                )
    for k in range(width // LANES):
        state = terms[k, strided(SUB - 1, steps), :]
        factor = jnp.ones_like(state)
        states, factors = [state], [factor]
        for s in range(SUB - 2, -1, -1):
            step_decay = decays[k, strided(s + 1, steps), :]
            state = terms[k, strided(s, steps), :] + step_decay * state
            factor = step_decay * factor
            states.append(state)
            factors.append(factor)
        first = decays[k, strided(0, steps), :]
        state, factor = first * state, first * factor
        carry = incoming[:, lanes(k)]
        entering = []
        for b in range(tiles - 1, -1, -1):
            entering.insert(0, carry)
            carry = state[b : b + 1, :] + factor[b : b + 1, :] * carry
        entering = jnp.concatenate(entering, axis=0)
        for s in range(SUB):
            terms[k, strided(SUB - 1 - s, steps), :] = states[s] + factors[s] * entering
        pulled_ref[:, lanes(k)] = (gains[k] * terms[k]).astype(jnp.bfloat16)


def image_kernel(
    region, b_ref, spatial, part_ref, direction_ref, residual_ref, image_ref, sums_ref
):
    _, width = b_ref.shape
    totals = [jnp.zeros((1, STRIP), jnp.float32) for _ in range(4)]
    for strip in range(width // STRIP):
        at = slice(strip * STRIP, (strip + 1) * STRIP)
        direction, residual = direction_ref[:, at], residual_ref[:, at]
        image = direction + (part_ref[:, at] + product(b_ref, 3, region, spatial, strip))
        image_ref[:, at] = image
        terms = (residual * residual, direction * image, residual * image, image * image)
        totals = [t + jnp.sum(term, axis=0, keepdims=True) for t, term in zip(totals, terms)]
    lane = lax.broadcasted_iota(jnp.int32, (1, LANES), 1)
    row = jnp.zeros((1, LANES), jnp.float32)
    for k, total in enumerate(totals):
        row = jnp.where(lane == k, jnp.sum(total, axis=1, keepdims=True), row)
    for device in range(sums_ref.shape[0]):
        sums_ref[device] = row


def update_kernel(
    totals_ref, solution_ref, residual_ref, direction_ref, image_ref, solution_new, residual_new, direction_new
):
    lane = lax.broadcasted_iota(jnp.int32, (1, LANES), 1)
    total = jnp.sum(totals_ref[...], axis=0)
    norm_old, curvature, cross_sum, image_sq = (
        jnp.sum(jnp.where(lane == k, total, 0.0), axis=1, keepdims=True) for k in range(4)
    )
    step_len = norm_old / curvature
    norm_new = norm_old - 2.0 * step_len * cross_sum + step_len * step_len * image_sq
    ratio = norm_new / norm_old
    for k in range(direction_ref.shape[1] // LANES):
        direction = direction_ref[:, lanes(k)]
        residual = residual_ref[:, lanes(k)] - step_len * image_ref[:, lanes(k)]
        solution_new[:, lanes(k)] = solution_ref[:, lanes(k)] + step_len * direction
        residual_new[:, lanes(k)] = residual
        direction_new[:, lanes(k)] = residual + ratio * direction


def body(
    solution,
    residual,
    direction,
    decay,
    spatial,
    tiles,
    tile_block,
    tile_time,
    tile_cell,
    tile_count,
    noise_inv,
):
    steps, width = direction.shape
    footprint = tiles[0, 0]
    capacity, soundings, cells = footprint.shape
    block_count = noise_inv.shape[0]
    here = lax.axis_index("tm").astype(jnp.int32).reshape(1)
    region = lax.axis_index("region").astype(jnp.int32).reshape(1)
    f32 = jnp.float32
    columns = pltpu.VMEM((width // LANES, steps, LANES), f32)
    regions = spatial.shape[1] // width
    devices = lax.axis_size("tm") * lax.axis_size("region")

    live = (jnp.arange(capacity, dtype=jnp.int32)[None] < tile_count).astype(jnp.int32)
    place = jnp.concatenate([tile_time[0], tile_cell[0], tile_block[0], live], axis=1)[0]
    half = direction.astype(jnp.bfloat16)
    blocks = region_blocks(half)
    part, prefix, decays, gains, last, kept = on_chip(
        prepare_kernel,
        [region],
        [blocks[0], blocks[1]],
        [((steps, width), f32)]
        + [(columns.shape, f32)] * 3
        + [((1, width), f32), (spatial.shape, spatial.dtype)],
        [pltpu.SemaphoreType.DMA((regions,)), pltpu.SemaphoreType.DMA((width // LANES,))],
        outside=[decay, spatial],
    )
    (part,) = on_chip(second_kernel, [region], [blocks[2], kept, part], [((steps, width), f32)])
    places = [place, shifted(place, "tm", -1), shifted(place, "tm", -2)]
    local, end = on_chip(
        filter_kernel,
        [region],
        [blocks[3], kept, part, decays, gains, last],
        [(columns.shape, f32), ((2, width), f32)],
    )
    own_rows, near_rows, far_rows = on_chip(
        gather_kernel, places, [local, prefix], [((2 * capacity, cells), f32)] * (BACK + 1)
    )
    near_rows = shifted(near_rows, "tm", 1)
    far_rows = shifted(far_rows, "tm", 2)
    ends = window_rows(end)
    seen, factors = on_chip(
        lambda *refs: observe_kernel(steps, len(ends), *refs),
        [here, place],
        [own_rows, near_rows, far_rows, footprint] + ends,
        [((block_count, soundings), f32), ((capacity, cells), f32)],
        [pltpu.VMEM((SUB, width), f32), pltpu.VMEM((capacity, cells), f32)],
    )
    bit = 1
    while bit < lax.axis_size("region") // 2:
        seen = seen + swapped(seen, "region", bit)
        bit *= 2
    rows, sums = on_chip(
        lambda *refs: adjoint_kernel(steps, *refs),
        [place],
        [seen, swapped(seen, "region", bit), noise_inv, footprint, factors],
        [((capacity, cells), f32), ((BACK + 2, width), f32)],
        [pltpu.VMEM(noise_inv.shape, f32)],
    )
    near_rows = shifted(rows, "tm", -1)
    far_rows = shifted(rows, "tm", -2)
    (pulled,) = on_chip(
        lambda *refs: hold_kernel(len(ends), *refs),
        [here] + places,
        [rows, near_rows, far_rows, decays, gains] + ends + window_rows(sums),
        [((steps, width), jnp.bfloat16)],
        [columns],
    )
    blocks = region_blocks(pulled)
    part, kept = on_chip(
        fetch_kernel,
        [region],
        [blocks[0], blocks[1]],
        [((steps, width), f32), (spatial.shape, spatial.dtype)],
        [pltpu.SemaphoreType.DMA((regions,))],
        outside=[spatial],
    )
    (part,) = on_chip(second_kernel, [region], [blocks[2], kept, part], [((steps, width), f32)])
    image, totals = on_chip(
        image_kernel,
        [region],
        [blocks[3], kept, part, direction, residual],
        [((steps, width), f32), ((devices, 1, LANES), f32)],
    )
    totals = lax.all_to_all(totals, ("tm", "region"), 0, 0, tiled=True)
    return on_chip(
        update_kernel,
        [],
        [totals, solution, residual, direction, image],
        [((steps, width), f32)] * 3,
        out_spaces=[jax.ShapeDtypeStruct] * 3,
    )


def solution(mesh):
    return jax.shard_map(
        body,
        mesh=mesh,
        in_specs=(
            P("tm", "region"),
            P("tm", "region"),
            P("tm", "region"),
            P("tm", "region"),
            P("region", None),
            P("tm", "region", None, None, None),
            P("tm", "region", None),
            P("tm", "region", None),
            P("tm", "region", None),
            P("tm", "region"),
            P("tm", None),
        ),
        out_specs=(P("tm", "region"), P("tm", "region"), P("tm", "region")),
        check_vma=False,
    )
```

```python
import jax
import jax.numpy as jnp
from jax import lax
from jax.experimental import pallas as pl
from jax.experimental.pallas import tpu as pltpu
from jax.sharding import PartitionSpec as P


FB = 512
BACK = 2
STRIP = 256
SUB = 8
LANES = 128
KERNEL_VMEM = 12 * 2**20


def swapped(block, axis, bit):
    return lax.ppermute(block, axis, [(i, i ^ bit) for i in range(lax.axis_size(axis))])


def shifted(block, axis, distance):
    devices = range(lax.axis_size(axis))
    route = [(i - distance, i) for i in devices if i - distance in devices]
    return lax.ppermute(block, axis, route)


def region_blocks(block):
    blocks, bit = {0: block}, lax.axis_size("region") // 2
    while bit:
        blocks.update({k ^ bit: swapped(b, "region", bit) for k, b in list(blocks.items())})
        bit //= 2
    return blocks


def window_rows(rows):
    bit, pieces = 1, [rows]
    while bit < lax.axis_size("tm"):
        joined = jnp.concatenate(pieces, axis=0) if len(pieces) > 1 else rows
        pieces.append(swapped(joined, "tm", bit))
        bit *= 2
    return pieces


def nt_dot(a, b):
    return lax.dot_general(a, b, (((1,), (1,)), ((), ())), preferred_element_type=jnp.float32)


def strided(start, steps):
    return pl.ds(start, steps // SUB, stride=SUB)


def lanes(k):
    return slice(k * LANES, (k + 1) * LANES)


def on_chip(kernel, scalars, arrays, outs, scratch=(), out_spaces=None, outside=()):
    spaces = out_spaces or [pltpu.VMEM] * len(outs)
    call = pl.pallas_call(
        kernel,
        out_shape=tuple(space(shape, dtype) for space, (shape, dtype) in zip(spaces, outs)),
        in_specs=[pl.BlockSpec(memory_space=pltpu.SMEM)] * len(scalars)
        + [pl.BlockSpec(memory_space=pltpu.VMEM)] * len(arrays)
        + [pl.BlockSpec(memory_space=pl.ANY)] * len(outside),
        out_specs=tuple(pl.BlockSpec(memory_space=pltpu.VMEM) for _ in outs),
        scratch_shapes=list(scratch),
        compiler_params=pltpu.CompilerParams(vmem_limit_bytes=KERNEL_VMEM),
    )
    arrays = [pltpu.with_memory_space_constraint(a, pltpu.VMEM) for a in arrays]
    return call(
        *scalars,
        *arrays,
        *(pltpu.with_memory_space_constraint(a, pltpu.HBM) for a in outside),
    )


def slots_of(place):
    return (place.shape[0] - 1) // 3


def tile_at(place, slot, steps):
    time = place[slot]
    return time // steps, time % steps, place[slots_of(place) + slot] * (FB // LANES)


def product(block, place, region, spatial, strip):
    width = block.shape[1]
    columns = pl.ds(pl.multiple_of((region[0] ^ place) * width, width), width)
    return nt_dot(block[...], spatial[strip * STRIP : (strip + 1) * STRIP, columns])


def first_kernel(region, a_ref, b_ref, spatial, out_ref):
    for strip in range(out_ref.shape[1] // STRIP):
        out_ref[:, strip * STRIP : (strip + 1) * STRIP] = product(
            a_ref, 0, region, spatial, strip
        ) + product(b_ref, 1, region, spatial, strip)


def fetch(region, spatial_hbm, spatial, arrived):
    width = spatial.shape[1] // arrived.shape[0]
    copies = []
    for place in range(arrived.shape[0]):
        columns = pl.ds(pl.multiple_of((region[0] ^ place) * width, width), width)
        copies.append(
            pltpu.make_async_copy(
                spatial_hbm.at[:, columns], spatial.at[:, columns], arrived.at[place]
            )
        )
        copies[-1].start()
    return copies


def fetch_kernel(region, a_ref, b_ref, spatial_hbm, part_ref, spatial, arrived):
    copies = fetch(region, spatial_hbm, spatial, arrived)
    copies[0].wait()
    copies[1].wait()
    first_kernel(region, a_ref, b_ref, spatial, part_ref)
    for copy in copies[2:]:
        copy.wait()


def second_kernel(region, a_ref, spatial, part_ref, out_ref):
    for strip in range(out_ref.shape[1] // STRIP):
        at = slice(strip * STRIP, (strip + 1) * STRIP)
        out_ref[:, at] = part_ref[:, at] + product(a_ref, 2, region, spatial, strip)


def prepare_kernel(
    region,
    a_ref,
    b_ref,
    decay_hbm,
    spatial_hbm,
    part_ref,
    prefix_ref,
    decays_ref,
    gains_ref,
    last_ref,
    spatial,
    arrived,
    decay_arrived,
):
    steps, width = a_ref.shape
    tiles = steps // SUB
    decay_copies = []
    for k in range(width // LANES):
        decay_copies.append(
            pltpu.make_async_copy(
                decay_hbm.at[:, pl.ds(k * LANES, LANES)], decays_ref.at[k], decay_arrived.at[k]
            )
        )
        decay_copies[-1].start()
    copies = fetch(region, spatial_hbm, spatial, arrived)
    for k in range(width // LANES):
        decay_copies[k].wait()
        decay = decays_ref[k]
        gains_ref[k] = jnp.sqrt(1.0 - decay * decay)
        running = [decays_ref[k, strided(0, steps), :]]
        for s in range(1, SUB):
            running.append(running[-1] * decays_ref[k, strided(s, steps), :])
        state = jnp.ones((1, LANES), jnp.float32)
        carried = []
        for b in range(tiles):
            carried.append(state)
            state = state * running[-1][b : b + 1, :]
        last_ref[:, lanes(k)] = state
        carried = jnp.concatenate(carried, axis=0)
        for s in range(SUB):
            prefix_ref[k, strided(s, steps), :] = running[s] * carried
    copies[0].wait()
    copies[1].wait()
    first_kernel(region, a_ref, b_ref, spatial, part_ref)
    for copy in copies[2:]:
        copy.wait()


def filter_kernel(
    region, b_ref, spatial, part_ref, decays, gains, last_ref, local, end_ref
):
    steps, width = b_ref.shape
    tiles = steps // SUB
    end_ref[0:1, :] = last_ref[...]
    for strip in range(width // STRIP):
        mixed = part_ref[:, strip * STRIP : (strip + 1) * STRIP] + product(
            b_ref, 3, region, spatial, strip
        )
        for k in range(strip * STRIP // LANES, (strip + 1) * STRIP // LANES):
            first = k * LANES - strip * STRIP
            local[k] = gains[k] * mixed[:, first : first + LANES]
            state = local[k, strided(0, steps), :]
            factor = decays[k, strided(0, steps), :]
            states, factors = [state], [factor]
            for s in range(1, SUB):
                step_decay = decays[k, strided(s, steps), :]
                state = step_decay * state + local[k, strided(s, steps), :]
                factor = step_decay * factor
                states.append(state)
                factors.append(factor)
            carry = jnp.zeros((1, LANES), jnp.float32)
            entering = []
            for b in range(tiles):
                entering.append(carry)
                carry = factor[b : b + 1, :] * carry + state[b : b + 1, :]
            end_ref[1:2, lanes(k)] = carry
            entering = jnp.concatenate(entering, axis=0)
            for s in range(SUB):
                local[k, strided(s, steps), :] = states[s] + factors[s] * entering


def gather_kernel(*refs):
    count = (len(refs) - 2) // 2
    local, prefix_ref = refs[count : count + 2]
    steps = local.shape[1]
    capacity = refs[-1].shape[0] // 2
    for place, rows_ref in zip(refs[:count], refs[count + 2 :]):
        for slot in range(capacity):
            _, step, first = tile_at(place, slot, steps)
            for k in range(FB // LANES):
                at = (first + k, pl.ds(step, 1))
                rows_ref[slot : slot + 1, lanes(k)] = local[*at, :]
                rows_ref[capacity + slot : capacity + slot + 1, lanes(k)] = prefix_ref[*at, :]


def lay_out(rows_ref, pieces):
    at = 0
    for piece in pieces:
        rows_ref[at : at + piece.shape[0], :] = piece[...]
        at += piece.shape[0]


def observe_kernel(steps, pieces, here, place, own_ref, near_ref, far_ref, tiles_ref, *rest):
    ends, (seen_ref, factor_ref, entered, picked, states) = rest[:pieces], rest[pieces:]
    capacity, soundings, cells = tiles_ref.shape
    windows = 2 ** (pieces - 1)
    width = ends[0].shape[1]
    own = here[0]
    entered[...] = jnp.zeros_like(entered)
    lay_out(states, ends)

    def one(window, state):
        for back in range(BACK + 1):

            @pl.when(window == own - back)
            def _():
                entered[BACK - back : BACK - back + 1, :] = state

        row = 2 * (window ^ own)
        return states[pl.ds(row, 1), :] * state + states[pl.ds(row + 1, 1), :]

    lax.fori_loop(0, windows, one, jnp.zeros((1, width), jnp.float32), unroll=windows <= 8)
    for slot in range(capacity):
        which, _, first = tile_at(place, slot, steps)
        columns = pl.ds(pl.multiple_of(first * LANES, FB), FB)
        row, later = slice(slot, slot + 1), slice(capacity + slot, capacity + slot + 1)
        offset = jnp.where(
            which == 2, own_ref[row, :], jnp.where(which == 1, near_ref[row, :], far_ref[row, :])
        )
        factor = jnp.where(
            which == 2, own_ref[later, :], jnp.where(which == 1, near_ref[later, :], far_ref[later, :])
        )
        factor_ref[row, :] = factor
        value = offset + factor * entered[pl.ds(which, 1), columns]
        picked[row, :] = jnp.where(slot < place[3 * capacity], value, 0.0)
    rows = picked[...].astype(jnp.bfloat16)
    products = nt_dot(rows, tiles_ref[...].reshape(capacity * soundings, cells))
    blocks = lax.broadcasted_iota(jnp.int32, seen_ref.shape, 0)
    seen = jnp.zeros(seen_ref.shape, jnp.float32)
    for slot in range(capacity):
        part = products[slot : slot + 1, slot * soundings : (slot + 1) * soundings]
        seen = seen + jnp.where(blocks == place[2 * capacity + slot], part, 0.0)
    seen_ref[...] = seen


def adjoint_kernel(
    steps, place, seen_ref, other_ref, noise_ref, tiles_ref, factor_ref, rows_ref, sums_ref, weights
):
    capacity, soundings, cells = tiles_ref.shape
    observed = seen_ref[...] + other_ref[...]
    weights[...] = (observed * noise_ref[...]).astype(jnp.bfloat16).astype(jnp.float32)
    slots = lax.broadcasted_iota(jnp.int32, (capacity, soundings), 0)
    pieces = []
    for slot in range(capacity):
        picked = weights[pl.ds(place[2 * capacity + slot], 1), :]
        pieces.append(jnp.where((slots == slot) & (slot < place[3 * capacity]), picked, 0.0))
    spread = jnp.concatenate(pieces, axis=1).astype(jnp.bfloat16)
    rows = jnp.dot(
        spread,
        tiles_ref[...].reshape(capacity * soundings, cells),
        preferred_element_type=jnp.float32,
    )
    rows_ref[...] = rows
    handed = rows * factor_ref[...]
    sums_ref[...] = jnp.zeros_like(sums_ref)
    for slot in range(capacity):
        which, _, first = tile_at(place, slot, steps)
        columns = pl.ds(pl.multiple_of(first * LANES, FB), FB)
        at = pl.ds(which, 1)
        sums_ref[at, columns] = sums_ref[at, columns] + handed[slot : slot + 1, :]


def hold_local_kernel(
    own, near, far, own_ref, near_ref, far_ref, decays, gains, terms, slope_ref
):
    steps = terms.shape[1]
    width = terms.shape[0] * LANES
    tiles = steps // SUB
    capacity = own_ref.shape[0]
    terms[...] = jnp.zeros_like(terms)
    for reader, (place, rows) in enumerate(((own, own_ref), (near, near_ref), (far, far_ref))):
        for slot in range(capacity):
            which, step, first = tile_at(place, slot, steps)
            mine = (which == BACK - reader) & (slot < place[3 * capacity])
            step = pl.ds(step, 1)
            for k in range(FB // LANES):
                terms[first + k, step, :] = terms[first + k, step, :] + jnp.where(
                    mine, rows[slot : slot + 1, lanes(k)], 0.0
                )
    for k in range(width // LANES):
        state = terms[k, strided(SUB - 1, steps), :]
        factor = jnp.ones_like(state)
        states, factors = [state], [factor]
        for s in range(SUB - 2, -1, -1):
            step_decay = decays[k, strided(s + 1, steps), :]
            state = terms[k, strided(s, steps), :] + step_decay * state
            factor = step_decay * factor
            states.append(state)
            factors.append(factor)
        first = decays[k, strided(0, steps), :]
        state, factor = first * state, first * factor
        carry, passed = jnp.zeros((1, LANES), jnp.float32), jnp.ones((1, LANES), jnp.float32)
        entering, passing = [], []
        for b in range(tiles - 1, -1, -1):
            entering.insert(0, carry)
            passing.insert(0, passed)
            passed = factor[b : b + 1, :] * passed
            carry = state[b : b + 1, :] + factor[b : b + 1, :] * carry
        entering = jnp.concatenate(entering, axis=0)
        passing = jnp.concatenate(passing, axis=0)
        for s in range(SUB):
            at = strided(SUB - 1 - s, steps)
            gain = gains[k, at, :]
            terms[k, at, :] = gain * (states[s] + factors[s] * entering)
            slope_ref[k, at, :] = gain * (factors[s] * passing)


def hold_kernel(pieces, here, base_ref, slope_ref, *rest):
    ends, sums = rest[:pieces], rest[pieces : 2 * pieces]
    pulled_ref, states, arrivals = rest[2 * pieces :]
    width = pulled_ref.shape[1]
    windows = 2 ** (pieces - 1)
    me = here[0]
    per = sums[0].shape[0]
    lay_out(states, ends)
    lay_out(arrivals, sums)

    def one(hop, state):
        window = windows - 1 - hop
        arriving = jnp.zeros((1, width), jnp.float32)
        for ahead in range(BACK + 1):
            reader = jnp.minimum(window + ahead, windows - 1)
            arriving = arriving + jnp.where(
                window + ahead < windows,
                arrivals[pl.ds((reader ^ me) * per + BACK - ahead, 1), :],
                0.0,
            )
        passed = states[pl.ds(2 * (window ^ me), 1), :] * state + arriving
        return jnp.where(window > me, passed, state)

    incoming = lax.fori_loop(
        0, windows - 1, one, jnp.zeros((1, width), jnp.float32), unroll=windows <= 8
    )
    for k in range(width // LANES):
        pulled_ref[:, lanes(k)] = (base_ref[k] + slope_ref[k] * incoming[:, lanes(k)]).astype(
            jnp.bfloat16
        )


def image_kernel(
    region, b_ref, spatial, part_ref, direction_ref, residual_ref, image_ref, sums_ref
):
    _, width = b_ref.shape
    totals = [jnp.zeros((1, STRIP), jnp.float32) for _ in range(4)]
    for strip in range(width // STRIP):
        at = slice(strip * STRIP, (strip + 1) * STRIP)
        direction, residual = direction_ref[:, at], residual_ref[:, at]
        image = direction + (part_ref[:, at] + product(b_ref, 3, region, spatial, strip))
        image_ref[:, at] = image
        terms = (residual * residual, direction * image, residual * image, image * image)
        totals = [t + jnp.sum(term, axis=0, keepdims=True) for t, term in zip(totals, terms)]
    lane = lax.broadcasted_iota(jnp.int32, (1, LANES), 1)
    row = jnp.zeros((1, LANES), jnp.float32)
    for k, total in enumerate(totals):
        row = jnp.where(lane == k, jnp.sum(total, axis=1, keepdims=True), row)
    for device in range(sums_ref.shape[0]):
        sums_ref[device] = row


def update_kernel(
    totals_ref, solution_ref, residual_ref, direction_ref, image_ref, solution_new, residual_new, direction_new
):
    lane = lax.broadcasted_iota(jnp.int32, (1, LANES), 1)
    total = jnp.sum(totals_ref[...], axis=0)
    norm_old, curvature, cross_sum, image_sq = (
        jnp.sum(jnp.where(lane == k, total, 0.0), axis=1, keepdims=True) for k in range(4)
    )
    step_len = norm_old / curvature
    norm_new = norm_old - 2.0 * step_len * cross_sum + step_len * step_len * image_sq
    ratio = norm_new / norm_old
    for k in range(direction_ref.shape[1] // LANES):
        direction = direction_ref[:, lanes(k)]
        residual = residual_ref[:, lanes(k)] - step_len * image_ref[:, lanes(k)]
        solution_new[:, lanes(k)] = solution_ref[:, lanes(k)] + step_len * direction
        residual_new[:, lanes(k)] = residual
        direction_new[:, lanes(k)] = residual + ratio * direction


def body(
    solution,
    residual,
    direction,
    decay,
    spatial,
    tiles,
    tile_block,
    tile_time,
    tile_cell,
    tile_count,
    noise_inv,
):
    steps, width = direction.shape
    footprint = tiles[0, 0]
    capacity, soundings, cells = footprint.shape
    block_count = noise_inv.shape[0]
    here = lax.axis_index("tm").astype(jnp.int32).reshape(1)
    region = lax.axis_index("region").astype(jnp.int32).reshape(1)
    f32 = jnp.float32
    columns = pltpu.VMEM((width // LANES, steps, LANES), f32)
    regions = spatial.shape[1] // width
    windows = lax.axis_size("tm")
    devices = windows * lax.axis_size("region")

    place = jnp.concatenate([tile_time[0], tile_cell[0], tile_block[0], tile_count], axis=1)[0]
    half = direction.astype(jnp.bfloat16)
    blocks = region_blocks(half)
    part, prefix, decays, gains, last, kept = on_chip(
        prepare_kernel,
        [region],
        [blocks[0], blocks[1]],
        [((steps, width), f32)]
        + [(columns.shape, f32)] * 3
        + [((1, width), f32), (spatial.shape, spatial.dtype)],
        [pltpu.SemaphoreType.DMA((regions,)), pltpu.SemaphoreType.DMA((width // LANES,))],
        outside=[decay, spatial],
    )
    (part,) = on_chip(second_kernel, [region], [blocks[2], kept, part], [((steps, width), f32)])
    places = [place, shifted(place, "tm", -1), shifted(place, "tm", -2)]
    local, end = on_chip(
        filter_kernel,
        [region],
        [blocks[3], kept, part, decays, gains, last],
        [(columns.shape, f32), ((2, width), f32)],
    )
    rows = ((2 * capacity, cells), f32)
    own_rows, near_rows, far_rows = on_chip(
        gather_kernel, places, [local, prefix], [rows] * (BACK + 1)
    )
    near_rows = shifted(near_rows, "tm", 1)
    far_rows = shifted(far_rows, "tm", 2)
    ends = window_rows(end)
    seen, factors = on_chip(
        lambda *refs: observe_kernel(steps, len(ends), *refs),
        [here, place],
        [own_rows, near_rows, far_rows, footprint] + ends,
        [((block_count, soundings), f32), ((capacity, cells), f32)],
        [
            pltpu.VMEM((SUB, width), f32),
            pltpu.VMEM((capacity, cells), f32),
            pltpu.VMEM((2 * windows, width), f32),
        ],
    )
    bit = 1
    while bit < lax.axis_size("region") // 2:
        seen = seen + swapped(seen, "region", bit)
        bit *= 2
    rows, sums = on_chip(
        lambda *refs: adjoint_kernel(steps, *refs),
        [place],
        [seen, swapped(seen, "region", bit), noise_inv, footprint, factors],
        [((capacity, cells), f32), ((BACK + 2, width), f32)],
        [pltpu.VMEM(noise_inv.shape, f32)],
    )
    near_rows = shifted(rows, "tm", -1)
    far_rows = shifted(rows, "tm", -2)
    base, slope = on_chip(
        hold_local_kernel,
        places,
        [rows, near_rows, far_rows, decays, gains],
        [(columns.shape, f32)] * 2,
    )
    (pulled,) = on_chip(
        lambda *refs: hold_kernel(len(ends), *refs),
        [here],
        [base, slope] + ends + window_rows(sums),
        [((steps, width), jnp.bfloat16)],
        [
            pltpu.VMEM((2 * windows, width), f32),
            pltpu.VMEM(((BACK + 2) * windows, width), f32),
        ],
    )
    blocks = region_blocks(pulled)
    part, kept = on_chip(
        fetch_kernel,
        [region],
        [blocks[0], blocks[1]],
        [((steps, width), f32), (spatial.shape, spatial.dtype)],
        [pltpu.SemaphoreType.DMA((regions,))],
        outside=[spatial],
    )
    (part,) = on_chip(second_kernel, [region], [blocks[2], kept, part], [((steps, width), f32)])
    image, totals = on_chip(
        image_kernel,
        [region],
        [blocks[3], kept, part, direction, residual],
        [((steps, width), f32), ((devices, 1, LANES), f32)],
    )
    totals = lax.all_to_all(totals, ("tm", "region"), 0, 0, tiled=True)
    return on_chip(
        update_kernel,
        [],
        [totals, solution, residual, direction, image],
        [((steps, width), f32)] * 3,
        out_spaces=[jax.ShapeDtypeStruct] * 3,
    )


def solution(mesh):
    return jax.shard_map(
        body,
        mesh=mesh,
        in_specs=(
            P("tm", "region"),
            P("tm", "region"),
            P("tm", "region"),
            P("tm", "region"),
            P("region", None),
            P("tm", "region", None, None, None),
            P("tm", "region", None),
            P("tm", "region", None),
            P("tm", "region", None),
            P("tm", "region"),
            P("tm", None),
        ),
        out_specs=(P("tm", "region"), P("tm", "region"), P("tm", "region")),
        check_vma=False,
    )
```

```python
import jax
import jax.numpy as jnp
from jax import lax
from jax.experimental import pallas as pl
from jax.experimental.pallas import tpu as pltpu
from jax.sharding import PartitionSpec as P


FB = 512
BACK = 2
STRIP = 512
SUB = 8
LANES = 128
KERNEL_VMEM = 12 * 2**20


def swapped(block, axis, bit):
    return lax.ppermute(block, axis, [(i, i ^ bit) for i in range(lax.axis_size(axis))])


def shifted(block, axis, distance):
    devices = range(lax.axis_size(axis))
    route = [(i - distance, i) for i in devices if i - distance in devices]
    return lax.ppermute(block, axis, route)


def region_blocks(block):
    blocks, bit = {0: block}, lax.axis_size("region") // 2
    while bit:
        blocks.update({k ^ bit: swapped(b, "region", bit) for k, b in list(blocks.items())})
        bit //= 2
    return blocks


def direct_round(ends, first, second, distance):
    near = shifted(first, "tm", distance)
    far = shifted(second, "tm", 2 * distance)
    both = jnp.concatenate([far, near], axis=0)
    pieces, bit = [ends], 1
    while bit < lax.axis_size("tm"):
        joined = jnp.concatenate(pieces, axis=0) if len(pieces) > 1 else ends
        pieces.append(swapped(joined, "tm", bit))
        bit *= 2
    return jnp.concatenate(pieces, axis=0), near, both, both


def nt_dot(a, b):
    return lax.dot_general(a, b, (((1,), (1,)), ((), ())), preferred_element_type=jnp.float32)


def strided(start, steps):
    return pl.ds(start, steps // SUB, stride=SUB)


def lanes(k):
    return slice(k * LANES, (k + 1) * LANES)


def on_chip(kernel, scalars, arrays, outs, scratch=(), out_spaces=None, outside=()):
    spaces = out_spaces or [pltpu.VMEM] * len(outs)
    call = pl.pallas_call(
        kernel,
        out_shape=tuple(space(shape, dtype) for space, (shape, dtype) in zip(spaces, outs)),
        in_specs=[pl.BlockSpec(memory_space=pltpu.SMEM)] * len(scalars)
        + [pl.BlockSpec(memory_space=pltpu.VMEM)] * len(arrays)
        + [pl.BlockSpec(memory_space=pl.ANY)] * len(outside),
        out_specs=tuple(pl.BlockSpec(memory_space=pltpu.VMEM) for _ in outs),
        scratch_shapes=list(scratch),
        compiler_params=pltpu.CompilerParams(vmem_limit_bytes=KERNEL_VMEM),
    )
    arrays = [pltpu.with_memory_space_constraint(a, pltpu.VMEM) for a in arrays]
    return call(
        *scalars,
        *arrays,
        *(pltpu.with_memory_space_constraint(a, pltpu.HBM) for a in outside),
    )


def slots_of(place):
    return place.shape[0] // 3


def tile_at(place, slot, steps):
    time = place[slot]
    return time // steps, time % steps, place[slots_of(place) + slot] * (FB // LANES)


def product(block, place, region, spatial, strip):
    width = block.shape[1]
    columns = pl.ds(pl.multiple_of((region[0] ^ place) * width, width), width)
    return nt_dot(block[...], spatial[strip * STRIP : (strip + 1) * STRIP, columns])


def first_kernel(region, a_ref, b_ref, spatial, out_ref):
    for strip in range(out_ref.shape[1] // STRIP):
        out_ref[:, strip * STRIP : (strip + 1) * STRIP] = product(
            a_ref, 0, region, spatial, strip
        ) + product(b_ref, 1, region, spatial, strip)


def fetch(region, spatial_hbm, spatial, arrived):
    width = spatial.shape[1] // arrived.shape[0]
    copies = []
    for place in range(arrived.shape[0]):
        columns = pl.ds(pl.multiple_of((region[0] ^ place) * width, width), width)
        copies.append(
            pltpu.make_async_copy(
                spatial_hbm.at[:, columns], spatial.at[:, columns], arrived.at[place]
            )
        )
        copies[-1].start()
    return copies


def fetch_kernel(region, a_ref, b_ref, spatial_hbm, part_ref, spatial, arrived):
    copies = fetch(region, spatial_hbm, spatial, arrived)
    copies[0].wait()
    copies[1].wait()
    first_kernel(region, a_ref, b_ref, spatial, part_ref)
    for copy in copies[2:]:
        copy.wait()


def second_kernel(region, a_ref, spatial, part_ref, out_ref):
    for strip in range(out_ref.shape[1] // STRIP):
        at = slice(strip * STRIP, (strip + 1) * STRIP)
        out_ref[:, at] = part_ref[:, at] + product(a_ref, 2, region, spatial, strip)


def prepare_kernel(
    region,
    here,
    a_ref,
    b_ref,
    decay_hbm,
    spatial_hbm,
    part_ref,
    prefix_ref,
    decays_ref,
    gains_ref,
    last_ref,
    spatial,
    arrived,
    decay_arrived,
):
    steps, width = a_ref.shape
    tiles = steps // SUB
    decay_copies = []
    for k in range(width // LANES):
        decay_copies.append(
            pltpu.make_async_copy(
                decay_hbm.at[:, pl.ds(k * LANES, LANES)], decays_ref.at[k], decay_arrived.at[k]
            )
        )
        decay_copies[-1].start()
    copies = fetch(region, spatial_hbm, spatial, arrived)
    for k in range(width // LANES):
        decay_copies[k].wait()
        decay = decays_ref[k]
        gains_ref[k] = jnp.sqrt(1.0 - decay * decay)
        running = [decays_ref[k, strided(0, steps), :]]
        for s in range(1, SUB):
            running.append(running[-1] * decays_ref[k, strided(s, steps), :])
        state = jnp.ones((1, LANES), jnp.float32)
        carried = []
        for b in range(tiles):
            carried.append(state)
            state = state * running[-1][b : b + 1, :]
        last_ref[:, lanes(k)] = state
        carried = jnp.concatenate(carried, axis=0)
        for s in range(SUB):
            prefix_ref[k, strided(s, steps), :] = running[s] * carried
    copies[0].wait()
    copies[1].wait()
    first_kernel(region, a_ref, b_ref, spatial, part_ref)
    for copy in copies[2:]:
        copy.wait()


def filter_kernel(
    region, b_ref, spatial, part_ref, decays, gains, last_ref, local, end_ref
):
    steps, width = b_ref.shape
    tiles = steps // SUB
    end_ref[0, 0:1, :] = last_ref[...]
    for strip in range(width // STRIP):
        mixed = part_ref[:, strip * STRIP : (strip + 1) * STRIP] + product(
            b_ref, 3, region, spatial, strip
        )
        for k in range(strip * STRIP // LANES, (strip + 1) * STRIP // LANES):
            first = k * LANES - strip * STRIP
            local[k] = gains[k] * mixed[:, first : first + LANES]
            state = local[k, strided(0, steps), :]
            factor = decays[k, strided(0, steps), :]
            states, factors = [state], [factor]
            for s in range(1, SUB):
                step_decay = decays[k, strided(s, steps), :]
                state = step_decay * state + local[k, strided(s, steps), :]
                factor = step_decay * factor
                states.append(state)
                factors.append(factor)
            carry = jnp.zeros((1, LANES), jnp.float32)
            entering = []
            for b in range(tiles):
                entering.append(carry)
                carry = factor[b : b + 1, :] * carry + state[b : b + 1, :]
            end_ref[0, 1:2, lanes(k)] = carry
            entering = jnp.concatenate(entering, axis=0)
            for s in range(SUB):
                local[k, strided(s, steps), :] = states[s] + factors[s] * entering


def gather_kernel(own, near, far, local, prefix_ref, own_ref, near_ref, far_ref):
    steps = local.shape[1]
    width = own_ref.shape[2]
    for place, rows_ref in ((own, own_ref), (near, near_ref), (far, far_ref)):
        for slot in range(slots_of(place)):
            _, step, first = tile_at(place, slot, steps)
            for part, source in enumerate((local, prefix_ref)):
                outer, row, columns = packed(2 * slot + part, FB, width)
                for k in range(FB // LANES):
                    start = columns.start + k * LANES
                    rows_ref[outer, row, start : start + LANES] = source[first + k, pl.ds(step, 1), :]


def live_kernel(count, live_ref):
    slots = lax.broadcasted_iota(jnp.int32, live_ref.shape, 0)
    live_ref[...] = jnp.where(slots < count[0, 0], 1.0, 0.0)


def lay_out(rows_ref, pairs):
    for k in range(pairs.shape[0]):
        rows_ref[2 * k : 2 * k + 2, :] = pairs[k]


def packed(slot, cells, width):
    per_row = width // cells
    row = slot // per_row
    return row // 2, slice(row % 2, row % 2 + 1), slice(slot % per_row * cells, (slot % per_row + 1) * cells)


def observe_kernel(
    steps,
    here,
    place,
    own_ref,
    near_ref,
    wide_ref,
    across_ref,
    tiles_ref,
    live_ref,
    ends,
    seen_ref,
    factor_ref,
    entered,
    picked,
    states,
):
    capacity, soundings, cells = tiles_ref.shape
    windows, _, width = ends.shape
    own = here[0]
    half = own_ref.shape[0]
    entered[...] = jnp.zeros_like(entered)
    lay_out(states, ends)

    def one(window, state):
        for back in range(BACK + 1):

            @pl.when(window == own - back)
            def _():
                entered[BACK - back : BACK - back + 1, :] = state

        row = 2 * (window ^ own)
        return states[pl.ds(row, 1), :] * state + states[pl.ds(row + 1, 1), :]

    lax.fori_loop(0, windows, one, jnp.zeros((1, width), jnp.float32), unroll=windows <= 8)
    odd, upper = own % 2 == 1, own % 4 >= 2
    for slot in range(capacity):
        which, _, first = tile_at(place, slot, steps)
        columns = pl.ds(pl.multiple_of(first * LANES, FB), FB)
        pair = []
        for part in range(2):
            outer, row, at = packed(2 * slot + part, cells, width)
            far, before = (
                jnp.where(upper, wide_ref[outer + base, row, at], across_ref[outer + base, row, at])
                for base in (0, half)
            )
            before = jnp.where(odd, near_ref[outer, row, at], before)
            pair.append(
                jnp.where(which == 2, own_ref[outer, row, at], jnp.where(which == 1, before, far))
            )
        offset, factor = (jnp.where(own + which >= BACK, value, 0.0) for value in pair)
        factor_ref[slot : slot + 1, :] = factor
        picked[slot : slot + 1, :] = offset + factor * entered[pl.ds(which, 1), columns]
    picked[...] = jnp.where(live_ref[:, 0:1] > 0.0, picked[...], 0.0)
    rows = picked[...].astype(jnp.bfloat16)
    products = nt_dot(rows, tiles_ref[...].reshape(capacity * soundings, cells))
    blocks = lax.broadcasted_iota(jnp.int32, seen_ref.shape, 0)
    seen = jnp.zeros(seen_ref.shape, jnp.float32)
    for slot in range(capacity):
        part = products[slot : slot + 1, slot * soundings : (slot + 1) * soundings]
        seen = seen + jnp.where(blocks == place[2 * capacity + slot], part, 0.0)
    seen_ref[...] = seen


def adjoint_kernel(
    steps,
    place,
    seen_ref,
    other_ref,
    noise_ref,
    tiles_ref,
    factor_ref,
    live_ref,
    rows_ref,
    pairs_ref,
    weights,
    sums_ref,
):
    capacity, soundings, cells = tiles_ref.shape
    observed = seen_ref[...] + other_ref[...]
    weights[...] = (observed * noise_ref[...]).astype(jnp.bfloat16).astype(jnp.float32)
    slots = lax.broadcasted_iota(jnp.int32, (capacity, soundings), 0)
    pieces = []
    for slot in range(capacity):
        picked = weights[pl.ds(place[2 * capacity + slot], 1), :]
        pieces.append(jnp.where(slots == slot, picked, 0.0))
    spread = jnp.concatenate(pieces, axis=1).astype(jnp.bfloat16)
    rows = jnp.dot(
        spread,
        tiles_ref[...].reshape(capacity * soundings, cells),
        preferred_element_type=jnp.float32,
    )
    rows = jnp.where(live_ref[:, 0:1] > 0.0, rows, 0.0)
    width = rows_ref.shape[2]
    for slot in range(capacity):
        rows_ref[packed(slot, cells, width)] = rows[slot : slot + 1, :]
    handed = rows * factor_ref[...]
    sums_ref[...] = jnp.zeros_like(sums_ref)
    for slot in range(capacity):
        which, _, first = tile_at(place, slot, steps)
        columns = pl.ds(pl.multiple_of(first * LANES, FB), FB)
        at = pl.ds(which, 1)
        sums_ref[at, columns] = sums_ref[at, columns] + handed[slot : slot + 1, :]
    for k in range(pairs_ref.shape[0]):
        pairs_ref[k] = sums_ref[2 * k : 2 * k + 2, :]


def hold_local_kernel(
    windows,
    here,
    own,
    near,
    far,
    own_ref,
    near_ref,
    wide_ref,
    across_ref,
    decays,
    gains,
    terms,
    slope_ref,
):
    steps = terms.shape[1]
    width = terms.shape[0] * LANES
    tiles = steps // SUB
    half = own_ref.shape[0]
    me = here[0]
    even, lower = me % 2 == 0, me % 4 < 2
    terms[...] = jnp.zeros_like(terms)
    for reader, place in enumerate((own, near, far)):
        for slot in range(slots_of(place)):
            outer, row, at = packed(slot, FB, width)

            def later(base):
                return jnp.where(
                    lower, wide_ref[outer + base, row, at], across_ref[outer + base, row, at]
                )

            if reader == 0:
                value = own_ref[outer, row, at]
            elif reader == 1:
                value = jnp.where(even, near_ref[outer, row, at], later(half))
            else:
                value = later(0)
            which, step, first = tile_at(place, slot, steps)
            mine = (which == BACK - reader) & (me + reader < windows)
            step = pl.ds(step, 1)
            for k in range(FB // LANES):
                terms[first + k, step, :] = terms[first + k, step, :] + jnp.where(
                    mine, value[:, lanes(k)], 0.0
                )
    for k in range(width // LANES):
        state = terms[k, strided(SUB - 1, steps), :]
        factor = jnp.ones_like(state)
        states, factors = [state], [factor]
        for s in range(SUB - 2, -1, -1):
            step_decay = decays[k, strided(s + 1, steps), :]
            state = terms[k, strided(s, steps), :] + step_decay * state
            factor = step_decay * factor
            states.append(state)
            factors.append(factor)
        first = decays[k, strided(0, steps), :]
        state, factor = first * state, first * factor
        carry, passed = jnp.zeros((1, LANES), jnp.float32), jnp.ones((1, LANES), jnp.float32)
        entering, passing = [], []
        for b in range(tiles - 1, -1, -1):
            entering.insert(0, carry)
            passing.insert(0, passed)
            passed = factor[b : b + 1, :] * passed
            carry = state[b : b + 1, :] + factor[b : b + 1, :] * carry
        entering = jnp.concatenate(entering, axis=0)
        passing = jnp.concatenate(passing, axis=0)
        for s in range(SUB):
            at = strided(SUB - 1 - s, steps)
            gain = gains[k, at, :]
            terms[k, at, :] = gain * (states[s] + factors[s] * entering)
            slope_ref[k, at, :] = gain * (factors[s] * passing)


def hold_kernel(here, base_ref, slope_ref, ends, sums, pulled_ref, states, arrivals):
    width = pulled_ref.shape[1]
    windows = ends.shape[0]
    me = here[0]
    per = arrivals.shape[0] // windows
    lay_out(states, ends)
    lay_out(arrivals, sums)

    def one(hop, state):
        window = windows - 1 - hop
        arriving = jnp.zeros((1, width), jnp.float32)
        for ahead in range(BACK + 1):
            reader = jnp.minimum(window + ahead, windows - 1)
            arriving = arriving + jnp.where(
                window + ahead < windows,
                arrivals[pl.ds((reader ^ me) * per + BACK - ahead, 1), :],
                0.0,
            )
        passed = states[pl.ds(2 * (window ^ me), 1), :] * state + arriving
        return jnp.where(window > me, passed, state)

    incoming = lax.fori_loop(
        0, windows - 1, one, jnp.zeros((1, width), jnp.float32), unroll=windows <= 8
    )
    for k in range(width // LANES):
        pulled_ref[:, lanes(k)] = (base_ref[k] + slope_ref[k] * incoming[:, lanes(k)]).astype(
            jnp.bfloat16
        )


def image_kernel(
    region, b_ref, spatial, part_ref, direction_ref, residual_ref, image_ref, sums_ref
):
    _, width = b_ref.shape
    totals = [jnp.zeros((1, STRIP), jnp.float32) for _ in range(4)]
    for strip in range(width // STRIP):
        at = slice(strip * STRIP, (strip + 1) * STRIP)
        direction, residual = direction_ref[:, at], residual_ref[:, at]
        image = direction + (part_ref[:, at] + product(b_ref, 3, region, spatial, strip))
        image_ref[:, at] = image
        terms = (residual * residual, direction * image, residual * image, image * image)
        totals = [t + jnp.sum(term, axis=0, keepdims=True) for t, term in zip(totals, terms)]
    lane = lax.broadcasted_iota(jnp.int32, (1, LANES), 1)
    row = jnp.zeros((1, LANES), jnp.float32)
    for k, total in enumerate(totals):
        row = jnp.where(lane == k, jnp.sum(total, axis=1, keepdims=True), row)
    for device in range(sums_ref.shape[0]):
        sums_ref[device] = row


def update_kernel(
    totals_ref,
    solution_ref,
    residual_ref,
    direction_ref,
    image_ref,
    solution_out,
    residual_out,
    direction_out,
    solution_new,
    residual_new,
    direction_new,
    left,
):
    lane = lax.broadcasted_iota(jnp.int32, (1, LANES), 1)
    total = jnp.sum(totals_ref[...], axis=0)
    norm_old, curvature, cross_sum, image_sq = (
        jnp.sum(jnp.where(lane == k, total, 0.0), axis=1, keepdims=True) for k in range(4)
    )
    step_len = norm_old / curvature
    norm_new = norm_old - 2.0 * step_len * cross_sum + step_len * step_len * image_sq
    ratio = norm_new / norm_old
    bands = left.shape[0]
    height = direction_ref.shape[0] // bands
    copies = []
    for band in range(bands):
        at = pl.ds(band * height, height)
        direction = direction_ref[at, :]
        residual = residual_ref[at, :] - step_len * image_ref[at, :]
        solution_new[at, :] = solution_ref[at, :] + step_len * direction
        residual_new[at, :] = residual
        direction_new[at, :] = residual + ratio * direction
        for k, (new, out) in enumerate(
            (
                (solution_new, solution_out),
                (residual_new, residual_out),
                (direction_new, direction_out),
            )
        ):
            copies.append(pltpu.make_async_copy(new.at[at, :], out.at[at, :], left.at[band, k]))
            copies[-1].start()
    for copy in copies:
        copy.wait()


def body(
    solution,
    residual,
    direction,
    decay,
    spatial,
    tiles,
    tile_block,
    tile_time,
    tile_cell,
    tile_count,
    noise_inv,
):
    steps, width = direction.shape
    footprint = tiles[0, 0]
    capacity, soundings, cells = footprint.shape
    block_count = noise_inv.shape[0]
    here = lax.axis_index("tm").astype(jnp.int32).reshape(1)
    region = lax.axis_index("region").astype(jnp.int32).reshape(1)
    f32 = jnp.float32
    columns = pltpu.VMEM((width // LANES, steps, LANES), f32)
    regions = spatial.shape[1] // width
    windows = lax.axis_size("tm")
    devices = windows * lax.axis_size("region")

    place = jnp.concatenate([tile_time[0], tile_cell[0], tile_block[0]], axis=1)[0]
    half = direction.astype(jnp.bfloat16)
    blocks = region_blocks(half)
    part, prefix, decays, gains, last, kept = on_chip(
        prepare_kernel,
        [region, here],
        [blocks[0], blocks[1]],
        [((steps, width), f32)]
        + [(columns.shape, f32)] * 3
        + [((1, width), f32), (spatial.shape, spatial.dtype)],
        [pltpu.SemaphoreType.DMA((regions,)), pltpu.SemaphoreType.DMA((width // LANES,))],
        outside=[decay, spatial],
    )
    (part,) = on_chip(second_kernel, [region], [blocks[2], kept, part], [((steps, width), f32)])
    places = [place, shifted(place, "tm", -1), shifted(place, "tm", -2)]
    local, end = on_chip(
        filter_kernel,
        [region],
        [blocks[3], kept, part, decays, gains, last],
        [(columns.shape, f32), ((1, 2, width), f32)],
    )
    pairs = ((2 * capacity * cells // (2 * width), 2, width), f32)
    own_rows, near_rows, far_rows = on_chip(
        gather_kernel, places, [local, prefix], [pairs] * (BACK + 1)
    )
    own_rows, tile_count = lax.optimization_barrier((own_rows, tile_count))
    (live,) = on_chip(live_kernel, [tile_count], [], [((capacity, LANES), f32)])
    ends, near_rows, wide_rows, across_rows = direct_round(end, near_rows, far_rows, 1)
    seen, factors = on_chip(
        lambda *refs: observe_kernel(steps, *refs),
        [here, place],
        [own_rows, near_rows, wide_rows, across_rows, footprint, live, ends],
        [((block_count, soundings), f32), ((capacity, cells), f32)],
        [
            pltpu.VMEM((SUB, width), f32),
            pltpu.VMEM((capacity, cells), f32),
            pltpu.VMEM((2 * windows, width), f32),
        ],
    )
    bit = 1
    while bit < lax.axis_size("region") // 2:
        seen = seen + swapped(seen, "region", bit)
        bit *= 2
    rows, sums = on_chip(
        lambda *refs: adjoint_kernel(steps, *refs),
        [place],
        [seen, swapped(seen, "region", bit), noise_inv, footprint, factors, live],
        [((capacity * cells // (2 * width), 2, width), f32), (((BACK + 2) // 2, 2, width), f32)],
        [pltpu.VMEM(noise_inv.shape, f32), pltpu.VMEM((BACK + 2, width), f32)],
    )
    sums, near_rows, wide_rows, across_rows = direct_round(sums, rows, rows, -1)
    base, slope = on_chip(
        lambda *refs: hold_local_kernel(windows, *refs),
        [here] + places,
        [rows, near_rows, wide_rows, across_rows, decays, gains],
        [(columns.shape, f32)] * 2,
    )
    (pulled,) = on_chip(
        hold_kernel,
        [here],
        [base, slope, ends, sums],
        [((steps, width), jnp.bfloat16)],
        [
            pltpu.VMEM((2 * windows, width), f32),
            pltpu.VMEM(((BACK + 2) * windows, width), f32),
        ],
    )
    blocks = region_blocks(pulled)
    part, kept = on_chip(
        fetch_kernel,
        [region],
        [blocks[0], blocks[1]],
        [((steps, width), f32), (spatial.shape, spatial.dtype)],
        [pltpu.SemaphoreType.DMA((regions,))],
        outside=[spatial],
    )
    (part,) = on_chip(second_kernel, [region], [blocks[2], kept, part], [((steps, width), f32)])
    image, totals = on_chip(
        image_kernel,
        [region],
        [blocks[3], kept, part, direction, residual],
        [((steps, width), f32), ((devices, 1, LANES), f32)],
    )
    totals = lax.all_to_all(totals, ("tm", "region"), 0, 0, tiled=True)
    state = pltpu.VMEM((steps, width), f32)
    return pl.pallas_call(
        update_kernel,
        out_shape=[jax.ShapeDtypeStruct((steps, width), f32)] * 3,
        in_specs=[pl.BlockSpec(memory_space=pltpu.VMEM)] * 5,
        out_specs=[pl.BlockSpec(memory_space=pl.ANY)] * 3,
        scratch_shapes=[state] * 3 + [pltpu.SemaphoreType.DMA((4, 3))],
        compiler_params=pltpu.CompilerParams(vmem_limit_bytes=KERNEL_VMEM),
        name="update",
    )(
        *(
            pltpu.with_memory_space_constraint(a, pltpu.VMEM)
            for a in (totals, solution, residual, direction, image)
        )
    )


def solution(mesh):
    return jax.shard_map(
        body,
        mesh=mesh,
        in_specs=(
            P("tm", "region"),
            P("tm", "region"),
            P("tm", "region"),
            P("tm", "region"),
            P("region", None),
            P("tm", "region", None, None, None),
            P("tm", "region", None),
            P("tm", "region", None),
            P("tm", "region", None),
            P("tm", "region"),
            P("tm", None),
        ),
        out_specs=(P("tm", "region"), P("tm", "region"), P("tm", "region")),
        check_vma=False,
    )
```
